32 devices in a mesh: rep: 2 (over x), shard: 4 (over z), seq: 4 (over y, core).
Axes of the slice: x: 2, y: 2, z: 4, core: 2. Of those that a mesh axis runs over, the one named last changes fastest.
Arguments:
- x_img: bfloat16 [16, 896, 1536], P(('rep', 'shard'), 'seq'), may hold values from -6 to 6
- x_txt: bfloat16 [16, 128, 1536], P(('rep', 'shard'), 'seq'), may hold values from -6 to 6
- cond: bfloat16 [16, 1536], P('rep'), may hold values from -6 to 6
- counts: int32 [8], P(('rep', 'shard')), may hold values from 1 to 2, as said below
- ct_img: bfloat16 [16, 896, 1536], P(('rep', 'shard'), 'seq'), may hold values from -6 to 6
- ct_txt: bfloat16 [16, 128, 1536], P(('rep', 'shard'), 'seq'), may hold values from -6 to 6
- ada_w: bfloat16 [2, 1536, 9216], P(None, ('shard', 'seq')), may hold values from -0.15625 to 0.15625
- ada_b: bfloat16 [2, 9216], P(None, ('shard', 'seq')), may hold values from -4 to 4
- qkv_w: bfloat16 [2, 1536, 4608], P(None, ('shard', 'seq')), may hold values from -0.15625 to 0.15625
- qv_b: bfloat16 [2, 3072], P(None, ('shard', 'seq')), may hold values from -1.5 to 1.5
- proj_w: bfloat16 [2, 1536, 1536], P(None, ('shard', 'seq')), may hold values from -1.5 to 1.5
- proj_b: bfloat16 [2, 1536], P(None, ('shard', 'seq')), may hold values from -1.5 to 1.5
- fc1_w: bfloat16 [2, 1536, 6144], P(None, ('shard', 'seq')), may hold values from -0.15625 to 0.15625
- fc1_b: bfloat16 [2, 6144], P(None, ('shard', 'seq')), may hold values from -1.5 to 1.5
- fc2_w: bfloat16 [2, 6144, 1536], P(None, ('shard', 'seq')), may hold values from -0.078125 to 0.078125
- fc2_b: bfloat16 [2, 1536], P(None, ('shard', 'seq')), may hold values from -1.5 to 1.5
Outputs:
- y_img: bfloat16 [16, 896, 1536], P(('rep', 'shard'), 'seq')
- y_txt: bfloat16 [16, 128, 1536], P(('rep', 'shard'), 'seq')
- dx_img: float32 [16, 896, 1536], P(('rep', 'shard'), 'seq')
- dx_txt: float32 [16, 128, 1536], P(('rep', 'shard'), 'seq')
- d_cond: float32 [16, 1536], P('rep')
- g_ada_w: float32 [2, 1536, 9216], P(None, ('shard', 'seq'))
- g_ada_b: float32 [2, 9216], P(None, ('shard', 'seq'))
- g_qkv_w: float32 [2, 1536, 4608], P(None, ('shard', 'seq'))
- g_qv_b: float32 [2, 3072], P(None, ('shard', 'seq'))
- g_proj_w: float32 [2, 1536, 1536], P(None, ('shard', 'seq'))
- g_proj_b: float32 [2, 1536], P(None, ('shard', 'seq'))
- g_fc1_w: float32 [2, 1536, 6144], P(None, ('shard', 'seq'))
- g_fc1_b: float32 [2, 6144], P(None, ('shard', 'seq'))
- g_fc2_w: float32 [2, 6144, 1536], P(None, ('shard', 'seq'))
- g_fc2_b: float32 [2, 1536], P(None, ('shard', 'seq'))
The draws below stay inside these ranges and needn't reach their ends.
Inputs may be any that keep to these rules, and one draw needn't show every extreme that they name: `counts`: each of the 8 groups has between 1 and 2 live sequences; some group is full and some has one.
All inputs are finite; a program needn't handle non-finite values.
Results may differ from the reference program's by a relative error of at most 0.0165.
The reference program's roundings to bfloat16 on the way count: a program that leaves them out, or rounds other values in their place, can miss the bound.
Values may be sent and summed in bfloat16 or wider, within the bound.
No kernel may reach another device: no remote copies, remote signals or barrier semaphores. Data moves between devices by JAX's collectives and lax.ppermute only.
A program may use at most 640 MiB of HBM per device.

```python
import jax
import jax.numpy as jnp
from jax import lax

D = 1536
H = 24
HD = 64
FF = 6144
CAP = 2
IMG = 896
TXT = 128
GROUPS = 8
SEQS = 16


def draw_counts(key, part):
    first_key, second_key, third_key = jax.random.split(jax.random.fold_in(key, 17), 3)
    values = jax.random.randint(first_key, (GROUPS,), 1, CAP + 1)
    full_place = jax.random.randint(second_key, (), 0, GROUPS)
    single_place = (full_place + 1 + jax.random.randint(third_key, (), 0, GROUPS - 1)) % GROUPS
    values = values.at[full_place].set(CAP).at[single_place].set(1)
    return values.astype(jnp.int32)


def block_scale(rng, dims, cuts, least, largest):
    def one(axis_at, parts):
        draws = jax.random.uniform(jax.random.fold_in(jax.random.fold_in(rng, 6), axis_at), (parts,), jnp.float32, least / len(cuts), largest / len(cuts))
        return jnp.repeat(jnp.exp(draws), dims[axis_at] // parts).reshape((-1,) + (1,) * (len(dims) - axis_at - 1))

    factor_of = one(*cuts[0])
    for cut in cuts[1:]:
        factor_of = factor_of * one(*cut)
    return factor_of


def bell_draw(own_key, extent, scale, most, cuts=(), kind=jnp.bfloat16):
    level = block_scale(own_key, extent, cuts, -0.22, 0.18) if cuts else 1.0
    array = jax.random.normal(own_key, extent, jnp.float32) * scale * level
    return jnp.minimum(jnp.maximum(array, -most), most).astype(kind)


def setup_inputs(seed: int = 0) -> dict:
    seeds = jax.random.split(jax.random.key(seed), 17)
    x_img = bell_draw(seeds[0], (SEQS, IMG, D), 1.0, 6.0, ((0, 8), (1, 4)))
    x_txt = bell_draw(seeds[1], (SEQS, TXT, D), 1.0, 6.0, ((0, 8), (1, 4)))
    cond = bell_draw(seeds[2], (SEQS, D), 1.0, 6.0, ((0, 2),))
    counts = draw_counts(jax.random.fold_in(seeds[16], 71), 0)
    ct_img = bell_draw(seeds[4], (SEQS, IMG, D), 1.0, 6.0, ((0, 8), (1, 4)))
    ct_txt = bell_draw(seeds[5], (SEQS, TXT, D), 1.0, 6.0, ((0, 8), (1, 4)))
    ada_w = bell_draw(seeds[6], (2, D, 6 * D), D ** -0.5, 0.15625, ((1, 16),))
    ada_b = bell_draw(seeds[7], (2, 6 * D), 0.3, 4.0, ((1, 16),))
    qkv_w = bell_draw(seeds[8], (2, D, 3 * D), D ** -0.5, 0.15625, ((1, 16),))
    qv_b = bell_draw(seeds[9], (2, 2 * D), 0.1, 1.5, ((1, 16),))
    proj_w = bell_draw(seeds[10], (2, D, D), 16 ** -0.5, 1.5, ((1, 16),))
    proj_b = bell_draw(seeds[11], (2, D), 0.1, 1.5, ((1, 16),))
    fc1_w = bell_draw(seeds[12], (2, D, FF), D ** -0.5, 0.15625, ((1, 16),))
    fc1_b = bell_draw(seeds[13], (2, FF), 0.1, 1.5, ((1, 16),))
    fc2_w = bell_draw(seeds[14], (2, FF, D), FF ** -0.5, 0.078125, ((1, 16),))
    fc2_b = bell_draw(seeds[15], (2, D), 0.1, 1.5, ((1, 16),))
    return dict(x_img=x_img, x_txt=x_txt, cond=cond, counts=counts, ct_img=ct_img, ct_txt=ct_txt, ada_w=ada_w, ada_b=ada_b, qkv_w=qkv_w, qv_b=qv_b, proj_w=proj_w, proj_b=proj_b, fc1_w=fc1_w, fc1_b=fc1_b, fc2_w=fc2_w, fc2_b=fc2_b)


@jax.custom_vjp
def low(v):
    return lax.optimization_barrier(v.astype(jnp.bfloat16)).astype(jnp.float32)

@jax.custom_vjp
def low_back(v):
    return v

def low_keep(v):
    return (low(v), None)

def low_pass(kept, grad):
    return (grad,)

def back_keep(v):
    return (v, None)

def back_low(kept, grad):
    return (low(grad),)
low.defvjp(low_keep, low_pass)
low_back.defvjp(back_keep, back_low)

def normalize(values):
    centre = lax.optimization_barrier(jnp.mean(values, axis=-1, keepdims=True))
    offset = values - centre
    spread = lax.optimization_barrier(jnp.mean(offset * offset, axis=-1, keepdims=True))
    return offset * lax.rsqrt(spread + 1e-06)

def joint_attention(joint):
    highest = lax.Precision.HIGHEST
    length = joint.shape[0]
    block = 512 if length % 512 == 0 else length
    query_heads = joint[:, :D].reshape(length // block, block, H, HD)
    key_heads = joint[:, D:2 * D].reshape(length, H, HD)
    value_heads = joint[:, 2 * D:].reshape(length, H, HD)

    def one_block(query_block):
        raw_scores = low_back(jnp.einsum('qhd,khd->hqk', query_block, key_heads, precision=highest))
        weights = low(jax.nn.softmax(raw_scores * HD ** (-0.5), axis=-1))
        return jnp.einsum('hqk,khd->qhd', weights, value_heads, precision=highest)
    mixed_out = lax.map(jax.checkpoint(one_block), query_heads)
    return mixed_out.reshape(length, D)

def layer(weights, img_in, txt_in, cond_in):
    highest = lax.Precision.HIGHEST
    ada_w, ada_b, qkv_w, qv_b, proj_w, proj_b, fc1_w, fc1_b, fc2_w, fc2_b = weights
    silu_cond = low(jax.nn.silu(cond_in))
    inputs = (img_in, txt_in)
    modulations = []
    projections = []
    for stream in range(2):
        stream_mod = low_back(jnp.dot(silu_cond, ada_w[stream], precision=highest) + ada_b[stream]).reshape(6, D)
        normed = normalize(inputs[stream])
        hidden = low(normed * (1.0 + stream_mod[1]) + stream_mod[0])
        qkv_bias = jnp.concatenate([qv_b[stream, :D], jnp.zeros((D,), jnp.float32), qv_b[stream, D:]])
        projected = low_back(low(jnp.dot(hidden, qkv_w[stream], precision=highest) + qkv_bias))
        modulations.append(stream_mod)
        projections.append(projected)
    joint = jnp.concatenate([projections[1], projections[0]], axis=0)
    mixed_out = low_back(low(joint_attention(joint)))
    attn_parts = (mixed_out[TXT:], mixed_out[:TXT])
    results = []
    for stream in range(2):
        stream_mod = modulations[stream]
        attn_out = low_back(jnp.dot(attn_parts[stream], proj_w[stream], precision=highest) + proj_b[stream])
        after_attn = inputs[stream] + stream_mod[2] * attn_out
        hidden_two = low(normalize(after_attn) * (1.0 + stream_mod[4]) + stream_mod[3])
        pre_act = low_back(jnp.dot(hidden_two, fc1_w[stream], precision=highest) + fc1_b[stream])
        activated = low(jax.nn.gelu(pre_act, approximate=True))
        mlp_out = low_back(jnp.dot(activated, fc2_w[stream], precision=highest) + fc2_b[stream])
        results.append(after_attn + stream_mod[5] * mlp_out)
    return (results[0], results[1])

def reference(x_img, x_txt, cond, counts, ct_img, ct_txt, ada_w, ada_b, qkv_w, qv_b, proj_w, proj_b, fc1_w, fc1_b, fc2_w, fc2_b):
    weights = tuple((item.astype(jnp.float32) for item in (ada_w, ada_b, qkv_w, qv_b, proj_w, proj_b, fc1_w, fc1_b, fc2_w, fc2_b)))
    slot_index = jnp.arange(SEQS, dtype=jnp.int32) % CAP
    live_mask = (slot_index < jnp.repeat(counts, CAP, total_repeat_length=SEQS)).astype(jnp.float32)

    def one_sequence(totals, item):
        img_in, txt_in, cond_in, img_ct, txt_ct, alive = item
        outputs, pull = jax.vjp(layer, weights, img_in, txt_in, cond_in)
        grads = pull((img_ct * alive, txt_ct * alive))
        new_totals = tuple((total + grad for total, grad in zip(totals, grads[0])))
        return (new_totals, (outputs[0] * alive, outputs[1] * alive, grads[1], grads[2], grads[3]))
    zero_totals = tuple((jnp.zeros(item.shape, jnp.float32) for item in weights))
    items = (x_img.astype(jnp.float32), x_txt.astype(jnp.float32), cond.astype(jnp.float32), ct_img.astype(jnp.float32), ct_txt.astype(jnp.float32), live_mask)
    totals, stacked = lax.scan(one_sequence, zero_totals, items)
    y_img, y_txt, dx_img, dx_txt, d_cond = stacked
    return (y_img.astype(jnp.bfloat16), y_txt.astype(jnp.bfloat16), dx_img, dx_txt, d_cond, totals[0], totals[1], totals[2], totals[3], totals[4], totals[5], totals[6], totals[7], totals[8], totals[9])
```

```python
import jax
import jax.numpy as jnp
from jax import lax
from jax.experimental import pallas as pl
from jax.experimental.pallas import tpu as pltpu
from jax.sharding import Mesh, PartitionSpec as P

HD = 64
BF = jnp.bfloat16
F32 = jnp.float32
FLIP = ((0, 1), (1, 0))


def matmul(left, right, left_dim, right_dim):
    return lax.dot_general(
        left, right, (((left_dim,), (right_dim,)), ((), ())), preferred_element_type=F32
    )


def attend_forward_kernel(low_ref, high_ref, out_ref, lse_ref, *, heads, block, scale):
    length = low_ref.shape[1]
    width = heads * HD
    for half, ref in enumerate((low_ref, high_ref)):
        for head in range(heads):
            at = head * HD
            place = half * width + at
            keys = ref[0, :, width + at : width + at + HD]
            values_t = ref[0, :, 2 * width + at : 2 * width + at + HD].T

            def one(step, carry, ref=ref, at=at, place=place, keys=keys, values_t=values_t, row=half * heads + head):
                rows = pl.ds(pl.multiple_of(step * block, block), block)
                queries = ref[0, rows, at : at + HD]
                raw = matmul(keys, queries, 1, 1)
                top = jnp.max(raw, axis=0, keepdims=True)
                grown = jnp.exp((raw - top) * scale)
                total = jnp.sum(grown, axis=0, keepdims=True)
                weights = (grown * (1.0 / total)).astype(BF)
                mixed_t = matmul(values_t, weights, 1, 0)
                out_ref[0, rows, place : place + HD] = mixed_t.T.astype(BF)
                lse_ref[0, row : row + 1, rows] = top * scale + jnp.log(total)
                return carry

            lax.fori_loop(0, length // block, one, 0)


def attend_backward_kernel(
    low_ref, high_ref, lse_ref, grad_ref, low_out, high_out, key_sum, value_sum, *, heads, block, scale
):
    length = low_ref.shape[1]
    width = heads * HD
    for half, (ref, out) in enumerate(((low_ref, low_out), (high_ref, high_out))):
        for head in range(heads):
            at = head * HD
            place = half * width + at
            keys = ref[0, :, width + at : width + at + HD]
            values = ref[0, :, 2 * width + at : 2 * width + at + HD]
            keys_t = keys.T
            key_sum[...] = jnp.zeros_like(key_sum)
            value_sum[...] = jnp.zeros_like(value_sum)

            def one(
                step, carry, ref=ref, out=out, at=at, place=place, keys=keys, values=values, keys_t=keys_t,
                row=half * heads + head,
            ):
                rows = pl.ds(pl.multiple_of(step * block, block), block)
                queries = ref[0, rows, at : at + HD]
                grad = grad_ref[0, rows, place : place + HD]
                raw = matmul(keys, queries, 1, 1)
                prob = jnp.exp(raw * scale - lse_ref[0, row : row + 1, rows])
                value_sum[...] += matmul(prob.astype(BF), grad, 1, 0)
                grad_prob = matmul(values, grad, 1, 1)
                delta = jnp.sum(prob * grad_prob, axis=0, keepdims=True)
                grad_raw = (prob * (grad_prob - delta) * scale).astype(BF)
                key_sum[...] += matmul(grad_raw, queries, 1, 0)
                query_t = matmul(keys_t, grad_raw, 1, 0)
                out[0, rows, at : at + HD] = query_t.T.astype(BF)
                return carry

            lax.fori_loop(0, length // block, one, 0)
            out[0, :, width + at : width + at + HD] = key_sum[...].astype(BF)
            out[0, :, 2 * width + at : 2 * width + at + HD] = value_sum[...].astype(BF)


def query_block(length):
    return 256 if length % 256 == 0 else length


def attend_forward(low, high):
    seqs, length, cols = low.shape
    heads = cols // (3 * HD)
    flops = 2 * 2 * heads * seqs * length * length * HD * 2
    spec = pl.BlockSpec((1, length, cols), lambda s: (s, 0, 0))
    return pl.pallas_call(
        lambda *refs: attend_forward_kernel(*refs, heads=heads, block=query_block(length), scale=HD**-0.5),
        grid=(seqs,),
        in_specs=[spec, spec],
        out_specs=[
            pl.BlockSpec((1, length, 2 * heads * HD), lambda s: (s, 0, 0)),
            pl.BlockSpec((1, 2 * heads, length), lambda s: (s, 0, 0)),
        ],
        out_shape=[
            jax.ShapeDtypeStruct((seqs, length, 2 * heads * HD), BF),
            jax.ShapeDtypeStruct((seqs, 2 * heads, length), F32),
        ],
        compiler_params=pltpu.CompilerParams(vmem_limit_bytes=40 << 20),
        cost_estimate=pl.CostEstimate(
            flops=4 * flops, bytes_accessed=2 * low.size * 2 * 2, transcendentals=seqs * 2 * heads * length * length
        ),
        name="attend_forward",
    )(low, high)


def attend_backward(low, high, lse, grad):
    seqs, length, cols = low.shape
    heads = cols // (3 * HD)
    flops = 5 * 2 * heads * seqs * length * length * HD * 2
    spec = pl.BlockSpec((1, length, cols), lambda s: (s, 0, 0))
    return pl.pallas_call(
        lambda *refs: attend_backward_kernel(*refs, heads=heads, block=query_block(length), scale=HD**-0.5),
        grid=(seqs,),
        in_specs=[
            spec,
            spec,
            pl.BlockSpec((1, 2 * heads, length), lambda s: (s, 0, 0)),
            pl.BlockSpec((1, length, 2 * heads * HD), lambda s: (s, 0, 0)),
        ],
        out_specs=[spec, spec],
        out_shape=[jax.ShapeDtypeStruct(low.shape, BF)] * 2,
        scratch_shapes=[pltpu.VMEM((length, HD), F32), pltpu.VMEM((length, HD), F32)],
        compiler_params=pltpu.CompilerParams(vmem_limit_bytes=40 << 20),
        cost_estimate=pl.CostEstimate(
            flops=4 * flops, bytes_accessed=4 * low.size * 2 * 2, transcendentals=seqs * 2 * heads * length * length
        ),
        name="attend_backward",
    )(low, high, lse, grad)


def swap(value, axis):
    return lax.ppermute(value, axis, FLIP)


def shift_xor(value, axis, bit):
    return lax.ppermute(value, axis, [(i, i ^ bit) for i in range(lax.axis_size(axis))])


def pick(index, first, second):
    return jnp.where(index == 0, first, second)


def paired(index, own, other, axis):
    return jnp.where(
        index == 0, jnp.concatenate([own, other], axis), jnp.concatenate([other, own], axis)
    )


def split_swap(value, dim, index, axis):
    first, second = jnp.split(value, 2, axis=dim)
    return pick(index, first, second), swap(pick(index, second, first), axis)


def spread(value, axes):
    value = value[None]
    for axis in reversed(axes):
        size, here = lax.axis_size(axis), lax.axis_index(axis)
        bit = 1
        while bit < size:
            value = paired((here // bit) % 2, value, shift_xor(value, axis, bit), 0)
            bit *= 2
    return value


def total(value, axes):
    for axis in axes:
        bit = 1
        while bit < lax.axis_size(axis):
            value = value + shift_xor(value, axis, bit)
            bit *= 2
    return value


def gather_square(own):
    half = own.shape[0] // 2
    from_x, from_y = swap(own, "x"), swap(own, "y")
    corner = jnp.concatenate([swap(from_x[:half], "y"), swap(from_y[half:], "x")], 0)
    return jnp.stack([own, from_y, from_x, corner])


def scatter_square(parts):
    half = parts.shape[1] // 2
    sent = parts[3].astype(BF)
    to_x = parts[2].at[:half].add(swap(sent[:half], "y").astype(F32)).astype(BF)
    to_y = parts[1].at[half:].add(swap(sent[half:], "x").astype(F32)).astype(BF)
    return parts[0] + swap(to_x, "x").astype(F32) + swap(to_y, "y").astype(F32)


def exchange_square(parts):
    own, for_y, for_x, for_corner = parts
    half = own.shape[0] // 2
    relay_y = swap(swap(for_corner[:half], "y"), "x")
    relay_x = swap(swap(for_corner[half:], "x"), "y")
    return [own, swap(for_y, "y"), swap(for_x, "x"), jnp.concatenate([relay_y, relay_x], 0)]


def on_device(
    x_img,
    x_txt,
    cond,
    counts,
    ct_img,
    ct_txt,
    ada_w,
    ada_b,
    qkv_w,
    qv_b,
    proj_w,
    proj_b,
    fc1_w,
    fc1_b,
    fc2_w,
    fc2_b,
):
    xi, yi, zi, ci = (lax.axis_index(name) for name in ("x", "y", "z", "c"))
    shards = lax.axis_size("z")
    owners = 4 * shards
    owner = zi * 4 + yi * 2 + ci
    width = x_img.shape[2]
    rows = ada_w.shape[1]
    part = width // 8
    rank_cols = width // 4
    ff_part = fc2_w.shape[1] // 2
    img = x_img.shape[1]
    txt = x_txt.shape[1]
    live = (ci < counts[0]).astype(F32)

    def to_slot(img_part, txt_part):
        both = jnp.concatenate([img_part, txt_part], 1)
        kept, received = split_swap(both, 0, ci, "c")
        return jnp.concatenate([kept, received], 0)

    tokens = to_slot(x_img, x_txt).astype(F32)

    cond_value = cond.astype(F32)
    silu_cond = jax.nn.silu(cond_value).astype(BF)
    silu_own = lax.dynamic_slice_in_dim(silu_cond, owner * rows, rows, 1)
    partial_mod = jnp.einsum("sd,jdm->jsm", silu_own, ada_w, preferred_element_type=F32)
    bias_full = lax.dynamic_update_slice_in_dim(
        jnp.zeros((2, 6 * width), F32), ada_b.astype(F32), owner * ada_b.shape[1], 1
    )
    mod = (partial_mod + bias_full[:, None]).reshape(2, shards, 2, 6 * width)
    kept, received = split_swap(mod, 2, ci, "c")
    mod = (kept + received)[:, :, 0]
    bit = shards // 2
    while bit >= 1:
        here = (zi // bit) % 2
        first, second = jnp.split(mod, 2, axis=1)
        mod = pick(here, first, second) + shift_xor(pick(here, second, first), "z", bit)
        bit //= 2
    mod = mod[:, 0]
    mod = (mod + swap(mod, "y")).reshape(2, 6, width)
    stream_of_row = (jnp.arange(img + txt) >= img)[None, :, None]

    def vector(index):
        return jnp.where(stream_of_row, mod[1, index], mod[0, index])

    small = jnp.concatenate([qv_b, proj_b, fc1_b, fc2_b], 1)
    small = spread(small, ("z", "y", "c"))
    cuts = [0]
    for item in (qv_b, proj_b, fc1_b, fc2_b):
        cuts.append(cuts[-1] + item.shape[1])
    qv_full, projb_full, upb_full, downb_full = (
        small[:, :, cuts[i] : cuts[i + 1]].transpose(1, 0, 2).reshape(2, -1).astype(F32) for i in range(4)
    )

    def at_rank(value, y_dim):
        value = lax.dynamic_index_in_dim(value, yi, y_dim, keepdims=False)
        return lax.dynamic_index_in_dim(value, xi, y_dim, keepdims=False)

    qv_rank = at_rank(qv_full.reshape(2, 2, 2, 2, 2, part), 2)
    qkv_bias = jnp.stack([qv_rank[:, 0], jnp.zeros_like(qv_rank[:, 0]), qv_rank[:, 1]], 2).reshape(2, 2, 3 * part)
    up_rank = upb_full.reshape(2, shards, 2, 2, 2, ff_part)
    up_rank = lax.dynamic_index_in_dim(up_rank, yi, 2, keepdims=False)
    up_rank = lax.dynamic_index_in_dim(up_rank, xi, 3, keepdims=False)
    up_bias = up_rank.transpose(0, 2, 1, 3).reshape(2, 2 * shards * ff_part)

    def column_weight(by_yc):
        cols = by_yc.shape[4]
        kept, received = split_swap(by_yc, 3, ci, "c")
        held = paired(ci, kept, received, 1)[:, :, :, 0]
        kept, received = split_swap(held, 2, yi, "y")
        held = paired(yi, kept, received, 1)[:, :, 0]
        full = lax.all_gather(held, ("c", "z"), axis=1, tiled=True)
        return full.reshape(2, 2, width, cols)

    qkv_x = lax.dynamic_index_in_dim(qkv_w.reshape(2, rows, 3, 2, 2, 2, part), xi, 4, keepdims=False)
    qkv_rank = column_weight(qkv_x.transpose(0, 1, 3, 4, 2, 5).reshape(2, rows, 2, 2, 3 * part))
    proj_full = lax.all_gather(proj_w, ("z", "y", "c"), axis=1, tiled=True)
    up_x = lax.dynamic_index_in_dim(fc1_w.reshape(2, rows, shards, 2, 2, 2, ff_part), xi, 5, keepdims=False)
    up_rank_w = column_weight(up_x.transpose(0, 1, 3, 4, 2, 5).reshape(2, rows, 2, 2, shards * ff_part))
    down_x = lax.dynamic_slice_in_dim(fc2_w, xi * ff_part, ff_part, 1)
    down_rank_w = lax.all_gather(down_x, ("c", "z"), axis=1, tiled=True)

    streams = (slice(0, img), slice(img, img + txt))

    def on_streams(value, weights, equation):
        return jnp.concatenate(
            [
                jnp.einsum(equation, value[..., cut, :], weights[j], preferred_element_type=F32)
                for j, cut in enumerate(streams)
            ],
            -2,
        )

    def with_bias(pair):
        return jnp.where(stream_of_row, pair[1], pair[0])

    def statistics(value):
        centre = jnp.mean(value, axis=-1, keepdims=True)
        offset = value - centre
        return offset, lax.rsqrt(jnp.mean(offset * offset, axis=-1, keepdims=True) + 1e-06)

    def back_normalize(grad, normed, scale):
        return scale * (
            grad
            - jnp.mean(grad, axis=-1, keepdims=True)
            - normed * jnp.mean(grad * normed, axis=-1, keepdims=True)
        )

    offset, spread_one = statistics(tokens)
    normed = offset * spread_one
    hidden = (normed * (1.0 + vector(1)) + vector(0)).astype(BF)
    hidden_all = gather_square(hidden)
    blocks = hidden_all.shape[1]
    seq_len = 2 * blocks * (img + txt)
    halves = []
    for half in range(2):
        value = on_streams(hidden_all, qkv_rank[:, half], "abtd,de->abte") + with_bias(qkv_bias[:, half])
        halves.append(value.astype(BF).reshape(2, seq_len, 3 * part))
    mixed, lse = attend_forward(halves[0], halves[1])
    mixed = mixed.reshape(4, blocks, img + txt, rank_cols)
    attn = jnp.concatenate(exchange_square([mixed[i] for i in range(4)]), -1)
    rank = 2 * yi + xi
    relative = [rank, rank ^ 2, rank ^ 1, rank ^ 3]
    proj_rel = jnp.concatenate(
        [lax.dynamic_slice_in_dim(proj_full, place * rank_cols, rank_cols, 1) for place in relative], 1
    )
    out = on_streams(attn, proj_rel, "btd,de->bte") + with_bias(projb_full)
    after = tokens + vector(2) * out

    offset_two, spread_two = statistics(after)
    normed_two = offset_two * spread_two
    hidden_two = (normed_two * (1.0 + vector(4)) + vector(3)).astype(BF)
    grad_y = to_slot(ct_img, ct_txt).astype(F32) * live
    grad_mlp = (vector(5) * grad_y).astype(BF)
    grad_mlp_all = gather_square(grad_mlp)
    hidden_two_all = gather_square(hidden_two)
    mlp_parts = []
    back_parts = []
    grad_up = []
    grad_down = []
    grad_upb = []
    for j, cut in enumerate(streams):
        hid = hidden_two_all[:, :, cut]
        top = grad_mlp_all[:, :, cut]
        up = up_rank_w[j]
        down = down_rank_w[j]
        pre = jnp.concatenate(
            [jnp.einsum("abtd,df->abtf", hid, up[h], preferred_element_type=F32) for h in range(2)], -1
        ) + up_bias[j]
        act, pull = jax.vjp(lambda v: jax.nn.gelu(v, approximate=True), pre)
        act = act.astype(BF)
        mlp_parts.append(jnp.einsum("abtf,fd->abtd", act, down, preferred_element_type=F32))
        grad_act = jnp.einsum("abtd,fd->abtf", top, down, preferred_element_type=F32)
        grad_pre = pull(grad_act)[0].astype(BF)
        split = grad_pre.shape[-1] // 2
        back_parts.append(
            jnp.einsum("abtf,df->abtd", grad_pre[..., :split], up[0], preferred_element_type=F32)
            + jnp.einsum("abtf,df->abtd", grad_pre[..., split:], up[1], preferred_element_type=F32)
        )
        grad_down.append(jnp.einsum("abtf,abtd->fd", act, top, preferred_element_type=F32).astype(BF))
        grad_up.append(
            jnp.stack(
                [
                    jnp.einsum("abtd,abtf->df", hid, piece, preferred_element_type=F32).astype(BF)
                    for piece in (grad_pre[..., :split], grad_pre[..., split:])
                ]
            )
        )
        grad_upb.append(jnp.sum(grad_pre.astype(F32), axis=(0, 1, 2)))
    mlp = scatter_square(jnp.concatenate(mlp_parts, -2)) + with_bias(downb_full)
    result = ((after + vector(5) * mlp) * live).astype(BF)
    grad_hidden_two = scatter_square(jnp.concatenate(back_parts, -2))

    def token_sums(value):
        return jnp.stack([jnp.sum(value[:, cut], axis=(0, 1)) for cut in streams])

    def to_owner(grad):
        cols = grad.shape[3]
        value = lax.psum_scatter(
            grad.reshape(2, 2 * shards, width // shards, cols), ("c", "z"), scatter_dimension=1, tiled=True
        ).reshape(2, 2, 2, rows, cols)
        kept, received = split_swap(value, 1, yi, "y")
        value = paired(yi, kept, received, 1)
        kept, received = split_swap(value, 2, ci, "c")
        value = paired(ci, kept, received, 2)
        value = value.transpose(0, 3, 1, 2, 4)[:, :, None]
        return paired(xi, value, swap(value, "x"), 2)

    def replicas(value):
        return lax.psum(value, "r") if lax.axis_size("r") > 1 else value

    up_owner = to_owner(jnp.stack(grad_up)).reshape(2, rows, 2, 2, 2, shards, ff_part)
    g_fc1_w = replicas(up_owner).transpose(0, 1, 5, 3, 4, 2, 6).reshape(fc1_w.shape).astype(F32)
    down_owner = lax.psum_scatter(jnp.stack(grad_down), ("c", "z"), scatter_dimension=1, tiled=True)
    g_fc2_w = replicas(paired(xi, down_owner, swap(down_owner, "x"), 1)).astype(F32)

    grad_after = grad_y + back_normalize(grad_hidden_two * (1.0 + vector(4)), normed_two, spread_two)
    grad_out = (vector(2) * grad_after).astype(BF)
    grad_attn = on_streams(grad_out, proj_rel, "bte,de->btd").astype(BF)
    grad_mixed = jnp.stack(
        exchange_square([grad_attn[..., i * rank_cols : (i + 1) * rank_cols] for i in range(4)])
    ).reshape(2, seq_len, rank_cols)
    grad_halves = attend_backward(halves[0], halves[1], lse, grad_mixed)
    grad_halves = [value.reshape(4, blocks, img + txt, 3 * part) for value in grad_halves]
    grad_hidden = scatter_square(
        on_streams(grad_halves[0], qkv_rank[:, 0], "abte,de->abtd")
        + on_streams(grad_halves[1], qkv_rank[:, 1], "abte,de->abtd")
    )
    grad_qkv = jnp.stack(
        [
            jnp.stack(
                [
                    jnp.einsum(
                        "abtd,abte->de", hidden_all[:, :, cut], value[:, :, cut], preferred_element_type=F32
                    ).astype(BF)
                    for value in grad_halves
                ]
            )
            for cut in streams
        ]
    )
    qkv_owner = to_owner(grad_qkv).reshape(2, rows, 2, 2, 2, 3, part)
    g_qkv_w = replicas(qkv_owner).transpose(0, 1, 5, 3, 2, 4, 6).reshape(qkv_w.shape).astype(F32)

    grad_proj = jnp.stack(
        [
            jnp.einsum("btd,bte->de", attn[:, cut], grad_out[:, cut], preferred_element_type=F32).astype(BF)
            for cut in streams
        ]
    )
    grad_proj = jnp.concatenate(
        [
            lax.dynamic_slice_in_dim(grad_proj, place * rank_cols, rank_cols, 1)
            for place in (
                (rank ^ t) * 0 + lax.select_n((rank ^ t), *[jnp.int32(v) for v in (0, 2, 1, 3)]) for t in range(4)
            )
        ],
        1,
    ).reshape(2, shards, 2, 2, rows, width)
    kept, received = split_swap(grad_proj, 3, ci, "c")
    grad_proj = (kept.astype(F32) + received.astype(F32)).astype(BF)
    kept, received = split_swap(grad_proj, 2, yi, "y")
    grad_proj = (kept.astype(F32) + received.astype(F32)).astype(BF).reshape(2, shards * rows, width)
    grad_proj = lax.psum_scatter(grad_proj, "z", scatter_dimension=1, tiled=True)
    g_proj_w = replicas(grad_proj.astype(F32) + swap(grad_proj, "x").astype(F32))

    grad_tokens = grad_after + back_normalize(grad_hidden * (1.0 + vector(1)), normed, spread_one)

    def from_slot(value):
        return paired(ci, value[:1], swap(value[1:], "c"), 0)

    result = from_slot(result)
    grad_tokens = from_slot(grad_tokens)

    sums = jnp.stack(
        [
            token_sums(grad_hidden),
            token_sums(grad_hidden * normed),
            token_sums(out * grad_after),
            token_sums(grad_hidden_two),
            token_sums(grad_hidden_two * normed_two),
            token_sums(mlp * grad_y),
        ],
        1,
    ).reshape(2, 6 * width)
    dmod = (sums + swap(sums, "y")).astype(BF)
    dmod_rep = spread(dmod, ("z", "c"))
    dsilu_part = jnp.einsum("sjm,jdm->sd", dmod_rep, ada_w, preferred_element_type=F32)
    dsilu = spread(dsilu_part, ("z", "y", "c")).transpose(1, 0, 2).reshape(2 * shards, owners * rows)
    gate = jax.nn.sigmoid(cond_value)
    d_cond = dsilu * gate * (1.0 + cond_value * (1.0 - gate))
    dmod_all = spread(dmod_rep, ("x",)).reshape(4 * shards, 2, 6 * width)
    silu_all = spread(silu_cond, ("x",)).reshape(4 * shards, width)
    if lax.axis_size("r") > 1:
        dmod_all = lax.all_gather(dmod_all, "r", axis=0, tiled=True)
        silu_all = lax.all_gather(silu_all, "r", axis=0, tiled=True)
    silu_cols = lax.dynamic_slice_in_dim(silu_all, owner * rows, rows, 1)
    g_ada_w = jnp.einsum("sd,sjm->jdm", silu_cols, dmod_all, preferred_element_type=F32)
    g_ada_b = lax.dynamic_slice_in_dim(
        jnp.sum(dmod_all.astype(F32), axis=0), owner * ada_b.shape[1], ada_b.shape[1], 1
    )

    here = ((jnp.arange(2)[:, None] == yi) & (jnp.arange(2)[None] == xi)).astype(F32)
    half_sums = jnp.stack(
        [
            jnp.stack([jnp.sum(value[:, :, cut].astype(F32), axis=(0, 1, 2)) for value in grad_halves])
            for cut in streams
        ]
    ).reshape(2, 2, 3, part)
    qv_sums = jnp.stack([half_sums[:, :, 0], half_sums[:, :, 2]], 1)
    qv_placed = (qv_sums[:, :, None, None] * here[:, :, None, None]).reshape(2, 2 * width)
    up_sums = jnp.stack(grad_upb).reshape(2, 2, shards, ff_part).transpose(0, 2, 1, 3)
    up_placed = (
        up_sums[:, :, None, :, None] * here[:, None, :, None]
    ).reshape(2, owners * 2 * ff_part)
    biases = jnp.concatenate(
        [qv_placed, token_sums(grad_out.astype(F32)), up_placed, token_sums(grad_mlp.astype(F32))], 1
    )
    biases = replicas(total(biases, ("c", "y", "x", "z")))
    g_biases = []
    start = 0
    for item in (qv_b, proj_b, fc1_b, fc2_b):
        cols = item.shape[1]
        g_biases.append(lax.dynamic_slice_in_dim(biases, start + owner * cols, cols, 1))
        start += owners * cols
    return (
        result[:, :img],
        result[:, img:],
        grad_tokens[:, :img],
        grad_tokens[:, img:],
        d_cond,
        g_ada_w,
        g_ada_b,
        g_qkv_w,
        g_biases[0],
        g_proj_w,
        g_biases[1],
        g_fc1_w,
        g_biases[2],
        g_fc2_w,
        g_biases[3],
    )


def solution(mesh):
    reps, shards, seqs = mesh.shape["rep"], mesh.shape["shard"], mesh.shape["seq"]
    fine = Mesh(mesh.devices.reshape(reps // 2, 2, shards, seqs // 2, 2), ("r", "x", "z", "y", "c"))
    group = ("r", "x", "z")
    token = P(group, ("y", "c"), None)
    cond = P(("r", "x"), None)
    matrix = P(None, ("z", "y", "c"), None)
    vector = P(None, ("z", "y", "c"))
    return jax.shard_map(
        on_device,
        mesh=fine,
        in_specs=(token, token, cond, P(group), token, token) + (matrix, vector) * 5,
        out_specs=(token, token, token, token, cond) + (matrix, vector) * 5,
        check_vma=False,
    )
```

```python
import jax
import jax.numpy as jnp
from jax import lax
from jax.experimental import pallas as pl
from jax.experimental.pallas import tpu as pltpu
from jax.sharding import Mesh, PartitionSpec as P

HD = 64
BF = jnp.bfloat16
F32 = jnp.float32
FLIP = ((0, 1), (1, 0))


def matmul(left, right, left_dim, right_dim):
    return lax.dot_general(
        left, right, (((left_dim,), (right_dim,)), ((), ())), preferred_element_type=F32
    )


def join_streams(img_ref, txt_ref, cut):
    img = img_ref[:, :, cut]
    txt = txt_ref[:, :, cut]
    return jnp.concatenate([img.reshape(-1, HD), txt.reshape(-1, HD)], 0)


def attend_forward_kernel(img_ref, txt_ref, out_ref, lse_ref, *, heads, scale):
    blocks = img_ref.shape[0]
    width = heads * HD
    rows = out_ref.shape[1]
    for head in range(heads):
        cut = slice(head * HD, head * HD + HD)
        keys = join_streams(img_ref, txt_ref, slice(width + cut.start, width + cut.stop))
        values_t = join_streams(img_ref, txt_ref, slice(2 * width + cut.start, 2 * width + cut.stop)).T
        for block in range(blocks):
            queries = jnp.concatenate([img_ref[block, :, cut], txt_ref[block, :, cut]], 0)
            raw = matmul(keys, queries, 1, 1)
            top = jnp.max(raw, axis=0, keepdims=True)
            grown = jnp.exp((raw - top) * scale)
            total = jnp.sum(grown, axis=0, keepdims=True)
            weights = (grown * (1.0 / total)).astype(BF)
            mixed_t = matmul(values_t, weights, 1, 0)
            out_ref[block, :, cut] = mixed_t.T.astype(BF)
            lse_ref[head : head + 1, block * rows : (block + 1) * rows] = top * scale + jnp.log(total)


def attend_backward_kernel(
    img_ref, txt_ref, lse_ref, grad_ref, img_out, txt_out, key_sum, value_sum, *, heads, scale
):
    blocks, img_rows = img_ref.shape[:2]
    txt_rows = txt_ref.shape[1]
    width = heads * HD
    rows = grad_ref.shape[1]
    for head in range(heads):
        cut = slice(head * HD, head * HD + HD)
        key_cut = slice(width + cut.start, width + cut.stop)
        value_cut = slice(2 * width + cut.start, 2 * width + cut.stop)
        keys = join_streams(img_ref, txt_ref, key_cut)
        values = join_streams(img_ref, txt_ref, value_cut)
        keys_t = keys.T
        for block in range(blocks):
            queries = jnp.concatenate([img_ref[block, :, cut], txt_ref[block, :, cut]], 0)
            grad = grad_ref[block, :, cut]
            raw = matmul(keys, queries, 1, 1)
            prob = jnp.exp(raw * scale - lse_ref[head : head + 1, block * rows : (block + 1) * rows])
            value_part = matmul(prob.astype(BF), grad, 1, 0)
            grad_prob = matmul(values, grad, 1, 1)
            delta = jnp.sum(prob * grad_prob, axis=0, keepdims=True)
            grad_raw = (prob * (grad_prob - delta) * scale).astype(BF)
            key_part = matmul(grad_raw, queries, 1, 0)
            if block == 0:
                value_sum[...] = value_part
                key_sum[...] = key_part
            else:
                value_sum[...] += value_part
                key_sum[...] += key_part
            grad_query = matmul(keys_t, grad_raw, 1, 0).T.astype(BF)
            img_out[block, :, cut] = grad_query[:img_rows]
            txt_out[block, :, cut] = grad_query[img_rows:]
        for there, total in ((key_cut, key_sum), (value_cut, value_sum)):
            for block in range(blocks):
                img_out[block, :, there] = total[block * img_rows : (block + 1) * img_rows].astype(BF)
                at = blocks * img_rows + block * txt_rows
                txt_out[block, :, there] = total[at : at + txt_rows].astype(BF)


def whole(shape):
    return pl.BlockSpec(shape, lambda: (0,) * len(shape))


def attend_cost(img, txt, heads, products):
    length = img.shape[0] * (img.shape[1] + txt.shape[1])
    return pl.CostEstimate(
        flops=products * 18 * heads * length * length * HD,
        bytes_accessed=4 * (img.size + txt.size),
        transcendentals=heads * length * length,
    )


def attend_forward(img, txt):
    blocks = img.shape[0]
    rows = img.shape[1] + txt.shape[1]
    heads = img.shape[2] // (3 * HD)
    outs = ((blocks, rows, heads * HD), (heads, blocks * rows))
    return pl.pallas_call(
        lambda *refs: attend_forward_kernel(*refs, heads=heads, scale=HD**-0.5),
        in_specs=[whole(img.shape), whole(txt.shape)],
        out_specs=[whole(shape) for shape in outs],
        out_shape=[jax.ShapeDtypeStruct(outs[0], BF), jax.ShapeDtypeStruct(outs[1], F32)],
        compiler_params=pltpu.CompilerParams(vmem_limit_bytes=40 << 20),
        cost_estimate=attend_cost(img, txt, heads, 2),
        name="attend_forward",
    )(img, txt)


def attend_backward(img, txt, lse, grad):
    heads = img.shape[2] // (3 * HD)
    length = img.shape[0] * (img.shape[1] + txt.shape[1])
    return pl.pallas_call(
        lambda *refs: attend_backward_kernel(*refs, heads=heads, scale=HD**-0.5),
        in_specs=[whole(value.shape) for value in (img, txt, lse, grad)],
        out_specs=[whole(img.shape), whole(txt.shape)],
        out_shape=[jax.ShapeDtypeStruct(img.shape, BF), jax.ShapeDtypeStruct(txt.shape, BF)],
        scratch_shapes=[pltpu.VMEM((length, HD), F32), pltpu.VMEM((length, HD), F32)],
        compiler_params=pltpu.CompilerParams(vmem_limit_bytes=40 << 20),
        cost_estimate=attend_cost(img, txt, heads, 5),
        name="attend_backward",
    )(img, txt, lse, grad)


CURVE = 0.7978845608028654
CUBIC = 0.044715


def gelu_and_slope(value):
    square = value * value
    bend = jnp.tanh(CURVE * value * (1.0 + CUBIC * square))
    rise = 0.5 + 0.5 * bend
    slope = rise + 0.5 * CURVE * value * (1.0 - bend * bend) * (1.0 + 3.0 * CUBIC * square)
    return value * rise, slope


def hidden_kernel(hid_ref, top_ref, up_ref, down_ref, bias_ref, act_ref, grad_ref):
    blocks, rows, width = hid_ref.shape
    cols = act_ref.shape[2]
    pre = matmul(hid_ref[...].reshape(blocks * rows, width), up_ref[...], 1, 0) + bias_ref[...]
    grad_act = matmul(top_ref[...].reshape(blocks * rows, width), down_ref[...], 1, 1)
    act, slope = gelu_and_slope(pre)
    act_ref[...] = act.astype(BF).reshape(blocks, rows, cols)
    grad_ref[...] = (grad_act * slope).astype(BF).reshape(blocks, rows, cols)


def output_kernel(act_ref, grad_ref, up_ref, down_ref, *refs):
    mlp_ref, back_ref = refs[-2:]
    blocks, rows, ff = act_ref.shape
    cols = mlp_ref.shape[2]
    back = matmul(grad_ref[...].reshape(blocks * rows, ff), up_ref[...], 1, 1)
    back_ref[...] = back.astype(BF).reshape(blocks, rows, cols)
    mlp = matmul(act_ref[...].reshape(blocks * rows, ff), down_ref[...], 1, 0)
    mlp_ref[...] = mlp.astype(BF).reshape(blocks, rows, cols)


def feed_forward_hidden(hid, top, up, down, bias, cut):
    blocks, _, width = hid.shape
    rows = cut.stop - cut.start
    ff = up.shape[1]
    tile = 256 if ff % 256 == 0 else ff
    token = pl.BlockSpec((blocks, rows, width), lambda f: (0, cut.start // rows, 0))
    out_spec = pl.BlockSpec((blocks, rows, tile), lambda f: (0, 0, f))
    size = blocks * rows
    return pl.pallas_call(
        hidden_kernel,
        grid=(ff // tile,),
        in_specs=[
            token,
            token,
            pl.BlockSpec((width, tile), lambda f: (0, f)),
            pl.BlockSpec((tile, width), lambda f: (f, 0)),
            pl.BlockSpec((1, tile), lambda f: (0, f)),
        ],
        out_specs=[out_spec, out_spec],
        out_shape=[jax.ShapeDtypeStruct((blocks, rows, ff), BF)] * 2,
        compiler_params=pltpu.CompilerParams(vmem_limit_bytes=48 << 20),
        cost_estimate=pl.CostEstimate(
            flops=8 * size * width * ff, bytes_accessed=4 * size * (width + ff) + 4 * up.size, transcendentals=size * ff
        ),
        name="feed_forward_hidden",
    )(hid, top, up, down, bias)


def feed_forward_output(act, grad_pre, up, down, cut, outs):
    blocks, rows, ff = act.shape
    width = up.shape[0]
    tile = 256 if width % 256 == 0 else width
    token = pl.BlockSpec((blocks, rows, ff), lambda n: (0, 0, 0))
    out_spec = pl.BlockSpec((blocks, rows, tile), lambda n: (0, cut.start // rows, n))
    filled = outs if isinstance(outs, (tuple, list)) else ()
    shape = filled[0].shape if filled else (blocks, outs, width)
    size = blocks * rows
    return pl.pallas_call(
        output_kernel,
        grid=(width // tile,),
        in_specs=[
            token,
            token,
            pl.BlockSpec((tile, ff), lambda n: (n, 0)),
            pl.BlockSpec((ff, tile), lambda n: (0, n)),
            *(pl.BlockSpec(memory_space=pl.ANY) for _ in filled),
        ],
        out_specs=[out_spec, out_spec],
        out_shape=[jax.ShapeDtypeStruct(shape, BF)] * 2,
        input_output_aliases={4: 0, 5: 1} if filled else {},
        compiler_params=pltpu.CompilerParams(vmem_limit_bytes=48 << 20),
        cost_estimate=pl.CostEstimate(
            flops=8 * size * width * ff, bytes_accessed=4 * size * (width + ff) + 4 * up.size, transcendentals=0
        ),
        name="feed_forward_output",
    )(act, grad_pre, up, down, *filled)


def swap(value, axis):
    return lax.ppermute(value, axis, FLIP)


def shift_xor(value, axis, bit):
    return lax.ppermute(value, axis, [(i, i ^ bit) for i in range(lax.axis_size(axis))])


def shift(value, axis, step):
    size = lax.axis_size(axis)
    return lax.ppermute(value, axis, [(i, (i + step) % size) for i in range(size)])


def swap_both(value):
    return lax.ppermute(value, ("x", "y"), [(i, 3 - i) for i in range(4)])


def pick(index, first, second):
    return jnp.where(index == 0, first, second)


def paired(index, own, other, axis):
    return jnp.where(
        index == 0, jnp.concatenate([own, other], axis), jnp.concatenate([other, own], axis)
    )


def split_swap(value, dim, index, axis):
    first, second = jnp.split(value, 2, axis=dim)
    return pick(index, first, second), swap(pick(index, second, first), axis)


def spread(value, axes):
    value = value[None]
    for axis in reversed(axes):
        size, here = lax.axis_size(axis), lax.axis_index(axis)
        bit = 1
        while bit < size:
            value = paired((here // bit) % 2, value, shift_xor(value, axis, bit), 0)
            bit *= 2
    return value


def total(value, axes):
    for axis in axes:
        bit = 1
        while bit < lax.axis_size(axis):
            value = value + shift_xor(value, axis, bit)
            bit *= 2
    return value


def after_these(values, others):
    leaves, tree = jax.tree.flatten(values)
    return jax.tree.unflatten(tree, lax.optimization_barrier((tuple(leaves), tuple(jax.tree.leaves(others))))[0])


def gather_square(own, beside=((), ())):
    from_x, from_y = after_these((swap(own, "x"), swap(own, "y")), beside[0])
    corner_a, corner_b = after_these((swap(from_x[:1], "y"), swap(from_y[1:], "x")), beside[1])
    return jnp.concatenate([own, from_y], 0), jnp.concatenate([from_x, corner_a, corner_b], 0)


def plus(first, second):
    return (first.astype(F32) + second.astype(F32)).astype(BF)


def relay_square(other):
    return swap(other[2:3], "y"), swap(other[3:4], "x")


def send_x(other, relays):
    return swap(plus(other[:1], relays[0]), "x"), swap(other[1:2], "x")


def send_y(own, relays):
    return swap(own[2:3], "y"), swap(plus(own[3:4], relays[1]), "y")


def sum_square(own, from_x, from_y):
    return own[:2].astype(F32) + jnp.concatenate(from_x, 0).astype(F32) + jnp.concatenate(from_y, 0).astype(F32)


def exchange_square(own, for_y, for_x, for_corner):
    return [own, swap(for_y, "y"), swap(for_x, "x"), swap_both(for_corner)]


def on_device(
    x_img,
    x_txt,
    cond,
    counts,
    ct_img,
    ct_txt,
    ada_w,
    ada_b,
    qkv_w,
    qv_b,
    proj_w,
    proj_b,
    fc1_w,
    fc1_b,
    fc2_w,
    fc2_b,
):
    xi, yi, zi, ci = (lax.axis_index(name) for name in ("x", "y", "z", "c"))
    shards = lax.axis_size("z")
    owners = 4 * shards
    owner = zi * 4 + yi * 2 + ci
    width = x_img.shape[2]
    rows = ada_w.shape[1]
    rank_cols = width // 4
    ff_block = fc2_w.shape[1]
    img = x_img.shape[1]
    txt = x_txt.shape[1]
    live = (ci < counts[0]).astype(F32)
    streams = (slice(0, img), slice(img, img + txt))

    def to_slot(img_part, txt_part):
        both = jnp.concatenate([img_part, txt_part], 1)
        kept, received = split_swap(both, 0, ci, "c")
        return jnp.concatenate([kept, received], 0)

    tokens = to_slot(x_img, x_txt).astype(F32)

    cotangents = to_slot(ct_img, ct_txt)
    ct_from_x, ct_from_y = swap(cotangents, "x"), swap(cotangents, "y")

    cond_value = cond.astype(F32)
    silu_cond = jax.nn.silu(cond_value).astype(BF)
    silu_own = lax.dynamic_slice_in_dim(silu_cond, owner * rows, rows, 1).reshape(shards, 2, rows)
    bias_full = lax.dynamic_update_slice_in_dim(
        jnp.zeros((2, 6 * width), F32), ada_b.astype(F32), owner * ada_b.shape[1], 1
    )

    def partial_mod(slots):
        return jnp.einsum("sd,jdm->sjm", slots, ada_w, preferred_element_type=F32) + bias_full

    mod_peer = partial_mod(pick(ci, silu_own[:, 1], silu_own[:, 0]))
    mod_sent = swap(mod_peer, "c")
    mod_own = partial_mod(pick(ci, silu_own[:, 0], silu_own[:, 1]))
    mod = mod_own + mod_sent
    mod_summed = mod
    mod_here = lax.dynamic_index_in_dim(mod, zi, 0, keepdims=False)
    for step in range(1, shards):
        there = lax.dynamic_index_in_dim(mod, (zi + step) % shards, 0, keepdims=False)
        mod_here = mod_here + shift(there, "z", step)
    mod = (mod_here + swap(mod_here, "y")).reshape(2, 6, width)
    stream_of_row = (jnp.arange(img + txt) >= img)[None, :, None]

    def vector(index):
        return jnp.where(stream_of_row, mod[1, index], mod[0, index])

    def with_bias(pair):
        return jnp.where(stream_of_row, pair[1], pair[0])

    def rank_columns(weight, offsets):
        by_y = [
            pick(
                xi,
                *(
                    jnp.concatenate([weight[:, :, at : at + size] for at, size in offsets(y, x)], 2)
                    for x in range(2)
                ),
            )
            for y in range(2)
        ]
        return pick(yi, by_y[0], by_y[1]), swap(pick(yi, by_y[1], by_y[0]), "y")

    def by_owner(kept, received):
        return jnp.stack([pick(yi, kept, received), pick(yi, received, kept)], 1)

    def natural_rows(gathered):
        cols = gathered.shape[3]
        return gathered.reshape(shards, 2, 2, rows, cols).transpose(0, 2, 1, 3, 4).reshape(width, cols)

    def qkv_offsets(y, x):
        return [(third * width + (2 * y + x) * rank_cols, rank_cols) for third in range(3)]

    def up_offsets(y, x):
        return [((z * 4 + y * 2 + x) * ff_block, ff_block) for z in range(shards)]

    qkv_pair = rank_columns(qkv_w, qkv_offsets)
    proj_swapped = swap(after_these(proj_w, qkv_pair[0]), "y")
    qkv_held = by_owner(*after_these(qkv_pair, mod_summed))
    qkv_gathered = lax.all_gather(qkv_held, ("z", "c"), axis=0)
    qkv_rank = [natural_rows(qkv_gathered[:, j]) for j in range(2)]

    def statistics(value):
        centre = jnp.mean(value, axis=-1, keepdims=True)
        offset = value - centre
        return offset, lax.rsqrt(jnp.mean(offset * offset, axis=-1, keepdims=True) + 1e-06)

    def back_normalize(grad, normed, scale):
        return scale * (
            grad
            - jnp.mean(grad, axis=-1, keepdims=True)
            - normed * jnp.mean(grad * normed, axis=-1, keepdims=True)
        )

    offset, spread_one = statistics(tokens)
    normed = offset * spread_one
    hidden = (normed * (1.0 + vector(1)) + vector(0)).astype(BF)
    hidden, ct_from_x, ct_from_y = after_these((hidden, ct_from_x, ct_from_y), (ct_from_x, ct_from_y))
    ct_corner = swap(ct_from_x[:1], "y"), swap(ct_from_y[1:], "x")
    gate_live = mod[:, 5] * live
    gate_other = swap(gate_live, "x")
    small = spread(jnp.concatenate(after_these((qv_b, proj_b, fc1_b, fc2_b), hidden), 1), ("y", "z", "c"))
    hidden_seqs = gather_square(hidden, (small, ct_corner))
    small = small.reshape(2, shards, 2, 2, -1).swapaxes(0, 1).reshape(owners, 2, -1)

    proj_held = by_owner(*after_these((proj_w, proj_swapped), (hidden, qkv_held)))
    fc1_w, fc2_w = after_these((fc1_w, fc2_w), hidden_seqs)
    up_pair = rank_columns(fc1_w, up_offsets)

    cuts = [0]
    for item in (qv_b, proj_b, fc1_b, fc2_b):
        cuts.append(cuts[-1] + item.shape[1])
    qv_full, projb_full, upb_full, downb_full = (
        small[:, :, cuts[i] : cuts[i + 1]].transpose(1, 0, 2).reshape(2, -1).astype(F32) for i in range(4)
    )

    def at_rank(pieces):
        return pick(yi, pick(xi, *pieces[0]), pick(xi, *pieces[1]))

    def rank_vector(value, offsets):
        return at_rank(
            [
                [jnp.concatenate([value[:, at : at + size] for at, size in offsets(y, x)], 1) for x in range(2)]
                for y in range(2)
            ]
        )

    qv_rank = rank_vector(qv_full, lambda y, x: qkv_offsets(y, x)[:2])
    qkv_bias = jnp.concatenate(
        [qv_rank[:, :rank_cols], jnp.zeros((2, rank_cols), F32), qv_rank[:, rank_cols:]], 1
    )
    up_bias = rank_vector(upb_full, up_offsets)

    proj_gathered = lax.all_gather(proj_held, ("z", "c"), axis=0).reshape(shards, 2, 2, 2, rows, width)
    def two_streams(value, weights, equation):
        return [
            jnp.einsum(equation, value[:, cut], weights[j], preferred_element_type=F32)
            for j, cut in enumerate(streams)
        ]

    halves = jnp.split(fc2_w, 2, axis=1)
    down_sent = swap(pick(ci, halves[1], halves[0]), "c")
    qkv_seqs, mixed_seqs, lse_seqs = [], [], []
    for value in hidden_seqs:
        if mixed_seqs:
            value = after_these(value, mixed_seqs)
        pair = [
            (item + qkv_bias[j]).astype(BF)
            for j, item in enumerate(two_streams(value, qkv_rank, "btd,de->bte"))
        ]
        mixed, lse = attend_forward(*pair)
        qkv_seqs.append(pair)
        mixed_seqs.append(mixed)
        lse_seqs.append(lse)
    up_held, down_sent = after_these((by_owner(*up_pair), down_sent), mixed_seqs[0])
    down_held = jnp.where(ci == xi, pick(ci, halves[0], halves[1]), down_sent)

    def gather_up(piece):
        return natural_rows(lax.all_gather(piece, ("z", "c"), axis=0))

    def gather_down(piece):
        return lax.all_gather(piece, ("z", "c"), axis=0, tiled=True)

    up_img = gather_up(up_held[0])
    down_img = gather_down(after_these(down_held[0], mixed_seqs[1]))
    attn = jnp.concatenate(
        exchange_square(mixed_seqs[0][:2], mixed_seqs[0][2:], mixed_seqs[1][:2], mixed_seqs[1][2:]), -1
    )
    up_rank = [up_img, gather_up(after_these(up_held[1], attn))]
    rank = 2 * yi + xi
    relative = (0, 2, 1, 3)
    proj_rel = [
        jnp.concatenate(
            [
                lax.dynamic_index_in_dim(proj_gathered, rank ^ flip, 0, keepdims=False)[:, j]
                .transpose(1, 0, 2, 3)
                .reshape(rank_cols, width)
                for flip in relative
            ],
            0,
        )
        for j in range(2)
    ]
    out = jnp.concatenate(two_streams(attn, proj_rel, "btd,de->bte"), 1) + with_bias(projb_full)
    after = tokens + vector(2) * out

    offset_two, spread_two = statistics(after)
    normed_two = offset_two * spread_two
    hidden_two = (normed_two * (1.0 + vector(4)) + vector(3)).astype(BF)
    grad_y = cotangents.astype(F32) * live

    def gated(gate, blocks):
        return (jnp.where(stream_of_row, gate[1], gate[0]) * jnp.concatenate(blocks, 0).astype(F32)).astype(BF)

    grad_mlp_seqs = [
        gated(gate_live, after_these((cotangents, ct_from_y), hidden_two)),
        gated(gate_other, after_these((ct_from_x, *ct_corner), hidden_two)),
    ]
    grad_mlp = grad_mlp_seqs[0][:2]
    down_rank = [down_img, gather_down(after_these(down_held[1], hidden_two))]
    hidden_two_seqs = gather_square(hidden_two)
    def hidden_of(j, hid, top):
        return feed_forward_hidden(hid, top, up_rank[j], down_rank[j], up_bias[j : j + 1], streams[j])

    act_img_other, pre_img_other = hidden_of(0, hidden_two_seqs[1], grad_mlp_seqs[1])
    outs_other = feed_forward_output(act_img_other, pre_img_other, up_img, down_img, streams[0], img + txt)
    act_img_own, pre_img_own = hidden_of(0, after_these(hidden_two_seqs[0], outs_other), grad_mlp_seqs[0])
    outs_own = feed_forward_output(act_img_own, pre_img_own, up_img, down_img, streams[0], img + txt)
    text_hids = after_these(hidden_two_seqs, outs_own)
    act_txt_other, pre_txt_other = hidden_of(1, text_hids[1], grad_mlp_seqs[1])
    mlp_other, back_other = feed_forward_output(
        act_txt_other, pre_txt_other, up_rank[1], down_rank[1], streams[1], outs_other
    )
    act_txt_own, pre_txt_own = hidden_of(1, after_these(text_hids[0], back_other), grad_mlp_seqs[0])
    mlp_own, back_own = feed_forward_output(act_txt_own, pre_txt_own, up_rank[1], down_rank[1], streams[1], outs_own)
    back_relays = after_these(relay_square(back_other), back_own)

    def replicas(value):
        return lax.psum(value, "r") if lax.axis_size("r") > 1 else value

    def two_sums(lefts, rights):
        first, second = (
            jnp.einsum("btd,bte->de", left, right, preferred_element_type=F32) for left, right in zip(lefts, rights)
        )
        return (first + second).astype(BF)

    def owner_rows(grad):
        cols = grad.shape[1]
        value = grad.reshape(shards, 2, 2, rows, cols).transpose(0, 2, 1, 3, 4).reshape(-1, cols)
        return lax.psum_scatter(value, ("z", "c"), scatter_dimension=0, tiled=True).reshape(2, rows, cols)

    def owner_columns(mine, others, offsets):
        by_rank = {}
        for y in range(2):
            for x in range(2):
                by_rank[y, x] = pick(
                    xi ^ x, pick(yi ^ y, mine[:, 0], mine[:, 1]), pick(yi ^ y, others[:, 0], others[:, 1])
                )
        places = []
        for (y, x), piece in by_rank.items():
            start = 0
            for at, size in offsets(y, x):
                places.append((at, piece[:, :, start : start + size].astype(F32)))
                start += size
        places.sort(key=lambda place: place[0])
        return jnp.concatenate([piece for _, piece in places], 2)

    cut = streams[0]
    down_grad_img = two_sums([act_img_own, act_img_other], [top[:, cut] for top in grad_mlp_seqs])
    up_grad_img = two_sums([hid[:, cut] for hid in hidden_two_seqs], [pre_img_own, pre_img_other])
    back_x, back_y = send_x(back_other, back_relays), send_y(back_own, back_relays)
    cut = streams[1]
    text = after_these((act_txt_own, act_txt_other, pre_txt_own, pre_txt_other), (back_own, back_relays))
    down_grad_txt = two_sums(text[:2], [top[:, cut] for top in grad_mlp_seqs])
    up_grad_txt = two_sums([hid[:, cut] for hid in hidden_two_seqs], text[2:])
    back_x, back_y = after_these((back_x, back_y), (down_grad_txt, up_grad_txt))
    grad_hidden_two = sum_square(back_own, back_x, back_y)
    grad_up = [owner_rows(up_grad_img), owner_rows(up_grad_txt)]
    grad_down = [
        lax.psum_scatter(down, ("z", "c"), scatter_dimension=0, tiled=True)
        for down in (down_grad_img, down_grad_txt)
    ]
    grad_after = grad_y + back_normalize(grad_hidden_two * (1.0 + vector(4)), normed_two, spread_two)
    grad_out = (vector(2) * grad_after).astype(BF)

    grad_attn = jnp.concatenate(
        [item.astype(BF) for item in two_streams(grad_out, proj_rel, "bte,de->btd")], 1
    )
    pieces = [grad_attn[:, :, i * rank_cols : (i + 1) * rank_cols] for i in range(4)]
    back = exchange_square(*pieces)
    grad_mixed_seqs = [jnp.concatenate(back[:2], 0), jnp.concatenate(back[2:], 0)]

    def hidden_back(grad_pair):
        return jnp.concatenate(
            [
                jnp.einsum("bte,de->btd", grad_pair[j], qkv_rank[j], preferred_element_type=F32).astype(BF)
                for j in range(2)
            ],
            1,
        )

    mlp_own, mlp_other = after_these((mlp_own, mlp_other), grad_mixed_seqs)
    mlp_relays = relay_square(mlp_other)
    mlp_x1, mlp_y2 = swap(mlp_other[1:2], "x"), swap(mlp_own[2:3], "y")
    grad_pair_other = attend_backward(*qkv_seqs[1], lse_seqs[1], grad_mixed_seqs[1])
    mlp_relays, mlp_x1, mlp_y2 = after_these((mlp_relays, mlp_x1, mlp_y2), grad_pair_other)
    hidden_back_other = hidden_back(after_these(grad_pair_other, mlp_relays))
    mlp_x0 = swap(plus(mlp_other[:1], mlp_relays[0]), "x")
    mlp_y3 = swap(plus(mlp_own[3:4], mlp_relays[1]), "y")

    grad_late = after_these(grad_out, hidden_back_other)
    position = lax.select_n(
        rank ^ jnp.arange(4), *(jnp.full((4,), place, jnp.int32) for place in (0, 2, 1, 3))
    )

    def proj_rows(core):
        blocks = [attn[:, :, at * rows : (at + 1) * rows] for at in range(16)]
        left = jnp.concatenate([pick(core, blocks[at], blocks[at + 1]) for at in range(0, 16, 2)], -1)
        return [
            jnp.einsum("btd,bte->de", left[:, cut], grad_late[:, cut], preferred_element_type=F32)
            .astype(BF)
            .reshape(4, 2, rows, width)
            for cut in streams
        ]

    proj_sent, proj_kept = jnp.stack(proj_rows(1 - ci)), jnp.stack(proj_rows(ci))
    proj_received = swap(proj_sent, "c")

    hidden_relays = relay_square(hidden_back_other)
    grad_pair_own = attend_backward(
        *qkv_seqs[0], lse_seqs[0], after_these(grad_mixed_seqs[0], (hidden_back_other, mlp_x1, mlp_y2, proj_kept))
    )
    hidden_relays = after_these(hidden_relays, grad_pair_own)
    mlp_x0, mlp_y3 = after_these((mlp_x0, mlp_y3), grad_pair_own)
    hidden_back_own = hidden_back(after_these(grad_pair_own, (hidden_relays, mlp_x0, mlp_y3)))
    mlp = sum_square(mlp_own, (mlp_x0, mlp_x1), (mlp_y2, mlp_y3)) + with_bias(downb_full)
    result = ((after + vector(5) * mlp) * live).astype(BF)
    hidden_x = send_x(hidden_back_other, hidden_relays)
    hidden_y = send_y(hidden_back_own, hidden_relays)

    def qkv_grad(j, pairs):
        return two_sums([hid[:, streams[j]] for hid in hidden_seqs], [pair[j] for pair in pairs])

    grad_pairs = [grad_pair_own, grad_pair_other]
    qkv_grad_img = qkv_grad(0, after_these(grad_pairs, hidden_back_own))
    hidden_x, hidden_y0 = after_these((hidden_x, hidden_y[0]), qkv_grad_img)
    qkv_grad_txt = qkv_grad(1, after_these(grad_pairs, hidden_y0))
    grad_qkv = jnp.stack([qkv_grad_img, qkv_grad_txt])
    cols = grad_qkv.shape[2]
    grad_qkv = grad_qkv.reshape(2, shards, 2, 2, rows, cols).transpose(1, 3, 0, 2, 4, 5)
    grad_qkv = grad_qkv.reshape(2 * shards, 2, 2, rows, cols)
    proj_received = after_these(proj_received, grad_qkv)
    grad_proj = plus(proj_kept, proj_received)
    grad_proj = jnp.concatenate([lax.dynamic_slice_in_dim(grad_proj, position[t], 1, 1) for t in range(4)], 1)
    proj_kept, proj_received = split_swap(grad_proj, 0, xi, "x")
    hidden_last = after_these(hidden_y[1], (grad_qkv, proj_kept))
    grad_hidden = sum_square(hidden_back_own, hidden_x, (hidden_y0, hidden_last))
    grad_qkv = lax.psum_scatter(grad_qkv, ("z", "c"), scatter_dimension=0, tiled=True).reshape(2, 2, rows, cols)

    up_pair = split_swap(replicas(after_these(jnp.stack(grad_up), grad_hidden)), 1, yi, "y")
    down = replicas(after_these(jnp.stack(grad_down), grad_hidden))
    down_other = swap(down, "x")
    grad_hidden_late = after_these(grad_hidden, (up_pair[0], down))

    grad_tokens = grad_after + back_normalize(grad_hidden * (1.0 + vector(1)), normed, spread_one)

    def from_slot(value):
        return paired(ci, value[:1], swap(value[1:], "c"), 0)

    result = from_slot(result)
    grad_tokens = from_slot(grad_tokens)

    def token_sums(value):
        return jnp.stack([jnp.sum(value[:, cut], axis=(0, 1)) for cut in streams])

    sums = jnp.stack(
        [
            token_sums(grad_hidden_late),
            token_sums(grad_hidden_late * normed),
            token_sums(out * grad_after),
            token_sums(grad_hidden_two),
            token_sums(grad_hidden_two * normed_two),
            token_sums(mlp * grad_y),
        ],
        1,
    ).reshape(2, 6 * width)
    up_pair, proj_received = after_these((up_pair, proj_received), sums)
    up_mine = jnp.concatenate(up_pair, 1)
    proj_kept, proj_received = split_swap(plus(proj_kept, proj_received)[0], 1, yi, "y")
    sums = after_these(sums, (up_mine, proj_kept))
    up_others = swap(up_mine, "x")
    dmod = (sums + swap(sums, "y")).astype(BF)
    dmod_rep = spread(dmod, ("z", "c"))
    qkv_pair = split_swap(replicas(grad_qkv), 1, yi, "y")
    up_others, late_pre, late_out, late_mlp, dmod_rep, down_other, proj_received = after_these(
        (
            up_others,
            (pre_img_own, pre_img_other, pre_txt_own, pre_txt_other),
            grad_out,
            grad_mlp,
            dmod_rep,
            down_other,
            proj_received,
        ),
        qkv_pair[0],
    )
    g_fc1_w = owner_columns(up_mine, up_others, up_offsets)
    grad_proj = plus(proj_kept, proj_received).reshape(shards * rows, width)
    grad_proj = replicas(lax.psum_scatter(grad_proj, "z", scatter_dimension=0, tiled=True))
    g_proj_w = paired(xi, grad_proj[None], swap(grad_proj, "x")[None], 0).astype(F32)
    blocks = (pick(xi, down, down_other), pick(xi, down_other, down))
    g_fc2_w = paired(ci, pick(ci, *blocks), swap(pick(ci, blocks[1], blocks[0]), "c"), 1).astype(F32)
    qkv_mine = jnp.concatenate(qkv_pair, 1)
    g_qkv_w = owner_columns(qkv_mine, swap(qkv_mine, "x"), qkv_offsets)
    dsilu_part = jnp.einsum("sjm,jdm->sd", dmod_rep, ada_w, preferred_element_type=F32)
    dsilu = spread(dsilu_part, ("z", "y", "c")).transpose(1, 0, 2).reshape(2 * shards, owners * rows)
    gate = jax.nn.sigmoid(cond_value)
    d_cond = dsilu * gate * (1.0 + cond_value * (1.0 - gate))
    dmod_all = spread(dmod_rep, ("x",)).reshape(4 * shards, 2, 6 * width)
    silu_all = spread(silu_cond, ("x",)).reshape(4 * shards, width)
    if lax.axis_size("r") > 1:
        dmod_all = lax.all_gather(dmod_all, "r", axis=0, tiled=True)
        silu_all = lax.all_gather(silu_all, "r", axis=0, tiled=True)
    silu_cols = lax.dynamic_slice_in_dim(silu_all, owner * rows, rows, 1)
    g_ada_w = jnp.einsum("sd,sjm->jdm", silu_cols, dmod_all, preferred_element_type=F32)
    g_ada_b = jnp.sum(
        lax.dynamic_slice_in_dim(dmod_all, owner * ada_b.shape[1], ada_b.shape[1], 2).astype(F32), axis=0
    )

    here = ((jnp.arange(2)[:, None] == yi) & (jnp.arange(2)[None] == xi)).astype(F32)
    qkv_sums = jnp.stack(
        [sum(jnp.sum(pair[j].astype(F32), axis=(0, 1)) for pair in grad_pairs) for j in range(2)]
    ).reshape(2, 3, rank_cols)
    qv_sums = jnp.stack([qkv_sums[:, 0], qkv_sums[:, 2]], 1)
    qv_placed = (qv_sums[:, :, None, None] * here[:, :, None]).reshape(2, 2 * width)
    up_sums = jnp.stack(
        [sum(jnp.sum(pre.astype(F32), axis=(0, 1)) for pre in late_pre[2 * j : 2 * j + 2]) for j in range(2)]
    ).reshape(2, shards, ff_block)
    up_placed = (up_sums[:, :, None, None] * here[:, :, None]).reshape(2, owners * ff_block)
    biases = jnp.concatenate(
        [qv_placed, token_sums(late_out.astype(F32)), up_placed, token_sums(late_mlp.astype(F32))], 1
    )
    biases = replicas(total(biases, ("c", "y", "x", "z")))
    g_biases = []
    start = 0
    for item in (qv_b, proj_b, fc1_b, fc2_b):
        cols = item.shape[1]
        g_biases.append(lax.dynamic_slice_in_dim(biases, start + owner * cols, cols, 1))
        start += owners * cols
    return (
        result[:, :img],
        result[:, img:],
        grad_tokens[:, :img],
        grad_tokens[:, img:],
        d_cond,
        g_ada_w,
        g_ada_b,
        g_qkv_w,
        g_biases[0],
        g_proj_w,
        g_biases[1],
        g_fc1_w,
        g_biases[2],
        g_fc2_w,
        g_biases[3],
    )


def solution(mesh):
    reps, shards, seqs = mesh.shape["rep"], mesh.shape["shard"], mesh.shape["seq"]
    fine = Mesh(mesh.devices.reshape(reps // 2, 2, shards, seqs // 2, 2), ("r", "x", "z", "y", "c"))
    group = ("r", "x", "z")
    token = P(group, ("y", "c"), None)
    cond = P(("r", "x"), None)
    matrix = P(None, ("z", "y", "c"), None)
    vector = P(None, ("z", "y", "c"))
    return jax.shard_map(
        on_device,
        mesh=fine,
        in_specs=(token, token, cond, P(group), token, token) + (matrix, vector) * 5,
        out_specs=(token, token, token, token, cond) + (matrix, vector) * 5,
        check_vma=False,
    )
```

```python
import jax
import jax.numpy as jnp
from jax import lax
from jax.experimental import pallas as pl
from jax.experimental.pallas import tpu as pltpu
from jax.sharding import Mesh, PartitionSpec as P

HD = 64
LOG2E = 1.4426950408889634
BF = jnp.bfloat16
F32 = jnp.float32
FLIP = ((0, 1), (1, 0))


def matmul(left, right, left_dim, right_dim):
    return lax.dot_general(
        left, right, (((left_dim,), (right_dim,)), ((), ())), preferred_element_type=F32
    )


def join_streams(img_ref, txt_ref, cut):
    img = img_ref[:, :, cut]
    txt = txt_ref[:, :, cut]
    return jnp.concatenate([img.reshape(-1, HD), txt.reshape(-1, HD)], 0)


def attend_forward_kernel(img_ref, txt_ref, out_ref, lse_ref, *, heads, scale):
    blocks = img_ref.shape[0]
    width = heads * HD
    rows = out_ref.shape[1]
    for head in range(heads):
        cut = slice(head * HD, head * HD + HD)
        keys = join_streams(img_ref, txt_ref, slice(width + cut.start, width + cut.stop))
        values_t = join_streams(img_ref, txt_ref, slice(2 * width + cut.start, 2 * width + cut.stop)).T
        for block in range(blocks):
            queries = jnp.concatenate([img_ref[block, :, cut], txt_ref[block, :, cut]], 0)
            raw = matmul(keys, queries, 1, 1) * scale
            top = jnp.max(raw, axis=0, keepdims=True)
            grown = jnp.exp2(raw - top)
            total = jnp.sum(grown, axis=0, keepdims=True)
            mixed_t = matmul(values_t, grown.astype(BF), 1, 0) * (1.0 / total)
            out_ref[block, :, cut] = mixed_t.T.astype(BF)
            lse_ref[head : head + 1, block * rows : (block + 1) * rows] = top + jnp.log2(total)


def attend_backward_kernel(
    img_ref, txt_ref, lse_ref, grad_ref, img_out, txt_out, key_sum, value_sum, *, heads, scale
):
    blocks, img_rows = img_ref.shape[:2]
    txt_rows = txt_ref.shape[1]
    width = heads * HD
    rows = grad_ref.shape[1]
    for head in range(heads):
        cut = slice(head * HD, head * HD + HD)
        key_cut = slice(width + cut.start, width + cut.stop)
        value_cut = slice(2 * width + cut.start, 2 * width + cut.stop)
        keys = join_streams(img_ref, txt_ref, key_cut)
        values = join_streams(img_ref, txt_ref, value_cut)
        keys_t = keys.T
        for block in range(blocks):
            queries = jnp.concatenate([img_ref[block, :, cut], txt_ref[block, :, cut]], 0)
            grad = grad_ref[block, :, cut]
            raw = matmul(keys, queries, 1, 1)
            prob = jnp.exp2(raw * scale - lse_ref[head : head + 1, block * rows : (block + 1) * rows])
            value_part = matmul(prob.astype(BF), grad, 1, 0)
            grad_prob = matmul(values, grad, 1, 1)
            delta = jnp.sum(prob * grad_prob, axis=0, keepdims=True)
            grad_raw = (prob * (grad_prob - delta)).astype(BF)
            key_part = matmul(grad_raw, queries, 1, 0)
            if block == 0:
                value_sum[...] = value_part
                key_sum[...] = key_part
            else:
                value_sum[...] += value_part
                key_sum[...] += key_part
            grad_query = (matmul(keys_t, grad_raw, 1, 0) * HD**-0.5).T.astype(BF)
            img_out[block, :, cut] = grad_query[:img_rows]
            txt_out[block, :, cut] = grad_query[img_rows:]
        for there, total, factor in ((key_cut, key_sum, HD**-0.5), (value_cut, value_sum, 1.0)):
            for block in range(blocks):
                img_out[block, :, there] = (total[block * img_rows : (block + 1) * img_rows] * factor).astype(BF)
                at = blocks * img_rows + block * txt_rows
                txt_out[block, :, there] = (total[at : at + txt_rows] * factor).astype(BF)


def whole(shape):
    return pl.BlockSpec(shape, lambda: (0,) * len(shape))


def attend_cost(img, txt, heads, products):
    length = img.shape[0] * (img.shape[1] + txt.shape[1])
    return pl.CostEstimate(
        flops=products * 18 * heads * length * length * HD,
        bytes_accessed=4 * (img.size + txt.size),
        transcendentals=heads * length * length,
    )


def attend_forward(img, txt):
    blocks = img.shape[0]
    rows = img.shape[1] + txt.shape[1]
    heads = img.shape[2] // (3 * HD)
    outs = ((blocks, rows, heads * HD), (heads, blocks * rows))
    return pl.pallas_call(
        lambda *refs: attend_forward_kernel(*refs, heads=heads, scale=HD**-0.5 * LOG2E),
        in_specs=[whole(img.shape), whole(txt.shape)],
        out_specs=[whole(shape) for shape in outs],
        out_shape=[jax.ShapeDtypeStruct(outs[0], BF), jax.ShapeDtypeStruct(outs[1], F32)],
        compiler_params=pltpu.CompilerParams(vmem_limit_bytes=40 << 20),
        cost_estimate=attend_cost(img, txt, heads, 2),
        name="attend_forward",
    )(img, txt)


def attend_backward(img, txt, lse, grad):
    heads = img.shape[2] // (3 * HD)
    length = img.shape[0] * (img.shape[1] + txt.shape[1])
    return pl.pallas_call(
        lambda *refs: attend_backward_kernel(*refs, heads=heads, scale=HD**-0.5 * LOG2E),
        in_specs=[whole(value.shape) for value in (img, txt, lse, grad)],
        out_specs=[whole(img.shape), whole(txt.shape)],
        out_shape=[jax.ShapeDtypeStruct(img.shape, BF), jax.ShapeDtypeStruct(txt.shape, BF)],
        scratch_shapes=[pltpu.VMEM((length, HD), F32), pltpu.VMEM((length, HD), F32)],
        compiler_params=pltpu.CompilerParams(vmem_limit_bytes=40 << 20),
        cost_estimate=attend_cost(img, txt, heads, 5),
        name="attend_backward",
    )(img, txt, lse, grad)


CURVE = 0.7978845608028654
CUBIC = 0.044715


def gelu_and_slope(value):
    square = value * value
    bend = jnp.tanh(CURVE * value * (1.0 + CUBIC * square))
    rise = 0.5 + 0.5 * bend
    slope = rise + 0.5 * CURVE * value * (1.0 - bend * bend) * (1.0 + 3.0 * CUBIC * square)
    return value * rise, slope


def rows_of(refs):
    values = [ref[...].reshape(-1, ref.shape[2]) for ref in refs]
    return values[0] if len(values) == 1 else jnp.concatenate(values, 0)


def store_rows(refs, value):
    start = 0
    for ref in refs:
        stop = start + ref.shape[0] * ref.shape[1]
        ref[...] = value[start:stop].reshape(ref.shape)
        start = stop


def hidden_kernel(*refs, count):
    hids, tops, (up_ref, down_ref, bias_ref) = refs[:count], refs[count : 2 * count], refs[2 * count : 2 * count + 3]
    acts, grads = refs[2 * count + 3 : 3 * count + 3], refs[3 * count + 3 :]
    pre = matmul(rows_of(hids), up_ref[...], 1, 0) + bias_ref[...]
    grad_act = matmul(rows_of(tops), down_ref[...], 1, 1)
    act, slope = gelu_and_slope(pre)
    store_rows(acts, act.astype(BF))
    store_rows(grads, (grad_act * slope).astype(BF))


def output_kernel(*refs, count):
    acts, grads, (up_ref, down_ref) = refs[:count], refs[count : 2 * count], refs[2 * count : 2 * count + 2]
    mlps, backs = refs[-2 * count : -count], refs[-count:]
    store_rows(backs, matmul(rows_of(grads), up_ref[...], 1, 1).astype(BF))
    store_rows(mlps, matmul(rows_of(acts), down_ref[...], 1, 0).astype(BF))


def feed_forward_hidden(hids, tops, up, down, bias, cut):
    count = len(hids)
    blocks, _, width = hids[0].shape
    rows = cut.stop - cut.start
    ff = up.shape[1]
    tile = 256 if ff % 256 == 0 else ff
    token = pl.BlockSpec((blocks, rows, width), lambda f: (0, cut.start // rows, 0))
    out_spec = pl.BlockSpec((blocks, rows, tile), lambda f: (0, 0, f))
    size = count * blocks * rows
    outs = pl.pallas_call(
        lambda *refs: hidden_kernel(*refs, count=count),
        grid=(ff // tile,),
        in_specs=[
            *[token] * (2 * count),
            pl.BlockSpec((width, tile), lambda f: (0, f)),
            pl.BlockSpec((tile, width), lambda f: (f, 0)),
            pl.BlockSpec((1, tile), lambda f: (0, f)),
        ],
        out_specs=[out_spec] * (2 * count),
        out_shape=[jax.ShapeDtypeStruct((blocks, rows, ff), BF)] * (2 * count),
        compiler_params=pltpu.CompilerParams(vmem_limit_bytes=48 << 20),
        cost_estimate=pl.CostEstimate(
            flops=8 * size * width * ff, bytes_accessed=4 * size * (width + ff) + 4 * up.size, transcendentals=size * ff
        ),
        name="feed_forward_hidden",
    )(*hids, *tops, up, down, bias)
    return outs[:count], outs[count:]


def feed_forward_output(acts, grads, up, down, cut, filled, all_rows):
    count = len(acts)
    blocks, rows, ff = acts[0].shape
    width = up.shape[0]
    tile = 256 if width % 256 == 0 else width
    token = pl.BlockSpec((blocks, rows, ff), lambda n: (0, 0, 0))
    out_spec = pl.BlockSpec((blocks, rows, tile), lambda n: (0, cut.start // rows, n))
    size = count * blocks * rows
    outs = pl.pallas_call(
        lambda *refs: output_kernel(*refs, count=count),
        grid=(width // tile,),
        in_specs=[
            *[token] * (2 * count),
            pl.BlockSpec((tile, ff), lambda n: (n, 0)),
            pl.BlockSpec((ff, tile), lambda n: (0, n)),
            *(pl.BlockSpec(memory_space=pl.ANY) for _ in filled),
        ],
        out_specs=[out_spec] * (2 * count),
        out_shape=[jax.ShapeDtypeStruct((blocks, all_rows, width), BF)] * (2 * count),
        input_output_aliases={2 * count + 2 + at: at for at in range(len(filled))},
        compiler_params=pltpu.CompilerParams(vmem_limit_bytes=48 << 20),
        cost_estimate=pl.CostEstimate(
            flops=8 * size * width * ff, bytes_accessed=4 * size * (width + ff) + 4 * up.size, transcendentals=0
        ),
        name="feed_forward_output",
    )(*acts, *grads, up, down, *filled)
    return outs[:count], outs[count:]


def weight_grad_kernel(*refs, count):
    lefts, rights, out_ref, turned = refs[:count], refs[count : 2 * count], refs[2 * count], refs[2 * count + 1]
    rows = lefts[0].shape[0] * lefts[0].shape[1]

    @pl.when(pl.program_id(0) == 0)
    def _():
        for at, left in enumerate(lefts):
            turned[:, at * rows : (at + 1) * rows] = left[...].reshape(rows, left.shape[2]).T

    total = matmul(turned[:, :rows], rights[0][...].reshape(rows, -1), 1, 0)
    for at in range(1, count):
        total = total + matmul(turned[:, at * rows : (at + 1) * rows], rights[at][...].reshape(rows, -1), 1, 0)
    out_ref[...] = total.astype(BF)


def weight_grad(lefts, rights, left_cut, right_cut):
    count = len(lefts)

    def rows_and_place(value, cut):
        rows = value.shape[1] if cut is None else cut.stop - cut.start
        return rows, 0 if cut is None else cut.start // rows

    blocks, _, left_cols = lefts[0].shape
    right_cols = rights[0].shape[2]
    rows, left_at = rows_and_place(lefts[0], left_cut)
    _, right_at = rows_and_place(rights[0], right_cut)
    tile = next(tile for tile in (512, 384, right_cols) if right_cols % tile == 0)
    tokens = count * blocks * rows
    return pl.pallas_call(
        lambda *refs: weight_grad_kernel(*refs, count=count),
        grid=(right_cols // tile,),
        in_specs=[
            *[pl.BlockSpec((blocks, rows, left_cols), lambda n: (0, left_at, 0))] * count,
            *[pl.BlockSpec((blocks, rows, tile), lambda n: (0, right_at, n))] * count,
        ],
        out_specs=pl.BlockSpec((left_cols, tile), lambda n: (0, n)),
        out_shape=jax.ShapeDtypeStruct((left_cols, right_cols), BF),
        scratch_shapes=[pltpu.VMEM((left_cols, tokens), BF)],
        compiler_params=pltpu.CompilerParams(vmem_limit_bytes=48 << 20),
        cost_estimate=pl.CostEstimate(
            flops=3 * tokens * left_cols * right_cols,
            bytes_accessed=2 * tokens * (left_cols + right_cols) + 2 * left_cols * right_cols,
            transcendentals=0,
        ),
        name="weight_grad",
    )(*lefts, *rights)


def owner_kernel(place_ref, mine_ref, others_ref, out_ref):
    take_mine = pl.program_id(1) % 2 == place_ref[0]
    out_ref[...] = jnp.where(take_mine, mine_ref[:, 0], others_ref[:, 0]).astype(F32)


def owner_columns(mine, others, xi, yi, parts):
    streams, _, rows, cols = mine.shape
    block = cols // parts
    place = jnp.stack([xi, yi]).astype(jnp.int32)
    spec = pl.BlockSpec(
        (streams, 1, rows, block), lambda part, rank, place: (0, (rank // 2 + place[1]) % 2, 0, part)
    )
    return pl.pallas_call(
        owner_kernel,
        grid_spec=pltpu.PrefetchScalarGridSpec(
            num_scalar_prefetch=1,
            grid=(parts, 4),
            in_specs=[spec, spec],
            out_specs=pl.BlockSpec((streams, rows, block), lambda part, rank, place: (0, 0, part * 4 + rank)),
        ),
        out_shape=jax.ShapeDtypeStruct((streams, rows, 4 * cols), F32),
        cost_estimate=pl.CostEstimate(flops=0, bytes_accessed=24 * mine.size, transcendentals=0),
        name="owner_columns",
    )(place, mine, others)


def swap(value, axis):
    return lax.ppermute(value, axis, FLIP)


def shift_xor(value, axis, bit):
    return lax.ppermute(value, axis, [(i, i ^ bit) for i in range(lax.axis_size(axis))])


def shift(value, axis, step):
    size = lax.axis_size(axis)
    return lax.ppermute(value, axis, [(i, (i + step) % size) for i in range(size)])


def swap_both(value):
    return lax.ppermute(value, ("x", "y"), [(i, 3 - i) for i in range(4)])


def pick(index, first, second):
    return jnp.where(index == 0, first, second)


def paired(index, own, other, axis):
    return jnp.where(
        index == 0, jnp.concatenate([own, other], axis), jnp.concatenate([other, own], axis)
    )


def split_swap(value, dim, index, axis):
    first, second = jnp.split(value, 2, axis=dim)
    return pick(index, first, second), swap(pick(index, second, first), axis)


def spread(value, axes):
    value = value[None]
    for axis in reversed(axes):
        size, here = lax.axis_size(axis), lax.axis_index(axis)
        bit = 1
        while bit < size:
            value = paired((here // bit) % 2, value, shift_xor(value, axis, bit), 0)
            bit *= 2
    return value


def total(value, axes):
    for axis in axes:
        bit = 1
        while bit < lax.axis_size(axis):
            value = value + shift_xor(value, axis, bit)
            bit *= 2
    return value


def together(values, others):
    return lax.optimization_barrier((values, others))


def gather_square(own):
    from_x, from_y = swap(own, "x"), swap(own, "y")
    corner_a, corner_b = swap(from_x[:1], "y"), swap(from_y[1:], "x")
    return jnp.concatenate([own, from_y], 0), jnp.concatenate([from_x, corner_a, corner_b], 0)


def plus(first, second):
    return (first.astype(F32) + second.astype(F32)).astype(BF)


def relay_square(other):
    return swap(other[2:3], "y"), swap(other[3:4], "x")


def send_x(other, relays):
    return swap(plus(other[:1], relays[0]), "x"), swap(other[1:2], "x")


def send_y(own, relays):
    return swap(own[2:3], "y"), swap(plus(own[3:4], relays[1]), "y")


def sum_square(own, from_x, from_y):
    return own[:2].astype(F32) + jnp.concatenate(from_x, 0).astype(F32) + jnp.concatenate(from_y, 0).astype(F32)


def exchange_square(own, for_y, for_x, for_corner):
    return [own, swap(for_y, "y"), swap(for_x, "x"), swap_both(for_corner)]


def on_device(
    x_img,
    x_txt,
    cond,
    counts,
    ct_img,
    ct_txt,
    ada_w,
    ada_b,
    qkv_w,
    qv_b,
    proj_w,
    proj_b,
    fc1_w,
    fc1_b,
    fc2_w,
    fc2_b,
):
    xi, yi, zi, ci = (lax.axis_index(name) for name in ("x", "y", "z", "c"))
    shards = lax.axis_size("z")
    owners = 4 * shards
    owner = zi * 4 + yi * 2 + ci
    width = x_img.shape[2]
    rows = ada_w.shape[1]
    rank_cols = width // 4
    ff_block = fc2_w.shape[1]
    img = x_img.shape[1]
    txt = x_txt.shape[1]
    live = (ci < counts[0]).astype(F32)
    streams = (slice(0, img), slice(img, img + txt))

    def to_slot(img_part, txt_part):
        both = jnp.concatenate([img_part, txt_part], 1)
        kept, received = split_swap(both, 0, ci, "c")
        return jnp.concatenate([kept, received], 0)

    tokens = to_slot(x_img, x_txt).astype(F32)

    cotangents = to_slot(ct_img, ct_txt)
    ct_from_x, ct_from_y = swap(cotangents, "x"), swap(cotangents, "y")

    cond_value = cond.astype(F32)
    silu_cond = jax.nn.silu(cond_value).astype(BF)
    silu_own = lax.dynamic_slice_in_dim(silu_cond, owner * rows, rows, 1).reshape(shards, 2, rows)
    bias_full = lax.dynamic_update_slice_in_dim(
        jnp.zeros((2, 6 * width), F32), ada_b.astype(F32), owner * ada_b.shape[1], 1
    )

    def partial_mod(slots):
        return jnp.einsum("sd,jdm->sjm", slots, ada_w, preferred_element_type=F32) + bias_full

    mod_peer = partial_mod(pick(ci, silu_own[:, 1], silu_own[:, 0]))
    mod_sent = swap(mod_peer, "c")
    mod_own = partial_mod(pick(ci, silu_own[:, 0], silu_own[:, 1]))
    mod = mod_own + mod_sent
    small = spread(jnp.concatenate([qv_b, proj_b, fc1_b, fc2_b], 1), ("z", "c", "y"))
    small, mod = together(small, mod)
    small = small.reshape(shards, 2, 2, 2, -1).swapaxes(1, 2).reshape(owners, 2, -1)
    mod_here = lax.dynamic_index_in_dim(mod, zi, 0, keepdims=False)
    for step in range(1, shards):
        there = lax.dynamic_index_in_dim(mod, (zi + step) % shards, 0, keepdims=False)
        mod_here = mod_here + shift(there, "z", step)
    mod = (mod_here + swap(mod_here, "y")).reshape(2, 6, width)
    stream_of_row = (jnp.arange(img + txt) >= img)[None, :, None]

    def vector(index):
        return jnp.where(stream_of_row, mod[1, index], mod[0, index])

    def with_bias(pair):
        return jnp.where(stream_of_row, pair[1], pair[0])

    def rank_columns(weight, offsets):
        by_y = [
            pick(
                xi,
                *(
                    jnp.concatenate([weight[:, :, at : at + size] for at, size in offsets(y, x)], 2)
                    for x in range(2)
                ),
            )
            for y in range(2)
        ]
        return pick(yi, by_y[0], by_y[1]), swap(pick(yi, by_y[1], by_y[0]), "y")

    def by_owner(kept, received):
        return jnp.stack([pick(yi, kept, received), pick(yi, received, kept)], 1)

    def natural_rows(gathered):
        cols = gathered.shape[3]
        return gathered.reshape(shards, 2, 2, rows, cols).transpose(0, 2, 1, 3, 4).reshape(width, cols)

    def qkv_offsets(y, x):
        return [(third * width + (2 * y + x) * rank_cols, rank_cols) for third in range(3)]

    def up_offsets(y, x):
        return [((z * 4 + y * 2 + x) * ff_block, ff_block) for z in range(shards)]

    qkv_pair = rank_columns(qkv_w, qkv_offsets)
    proj_swapped = swap(proj_w, "y")
    qkv_held = by_owner(*qkv_pair)
    qkv_gathered = lax.all_gather(qkv_held, ("z", "c"), axis=0)
    qkv_rank = [natural_rows(qkv_gathered[:, j]) for j in range(2)]

    def statistics(value):
        centre = jnp.mean(value, axis=-1, keepdims=True)
        offset = value - centre
        return offset, lax.rsqrt(jnp.mean(offset * offset, axis=-1, keepdims=True) + 1e-06)

    def back_normalize(grad, normed, scale):
        return scale * (
            grad
            - jnp.mean(grad, axis=-1, keepdims=True)
            - normed * jnp.mean(grad * normed, axis=-1, keepdims=True)
        )

    offset, spread_one = statistics(tokens)
    normed = offset * spread_one
    hidden = (normed * (1.0 + vector(1)) + vector(0)).astype(BF)
    gate_live = mod[:, 5] * live
    gate_other = swap(gate_live, "x")
    hidden_x, hidden_y = swap(hidden, "x"), swap(hidden, "y")
    (ct_from_x, ct_from_y), (hidden_x, hidden_y) = together((ct_from_x, ct_from_y), (hidden_x, hidden_y))
    hidden_corner = swap(hidden_x[:1], "y"), swap(hidden_y[1:], "x")
    ct_corner = swap(ct_from_x[:1], "y"), swap(ct_from_y[1:], "x")
    hidden_seqs = [
        jnp.concatenate([hidden, hidden_y], 0),
        jnp.concatenate([hidden_x, *hidden_corner], 0),
    ]

    proj_held = by_owner(proj_w, proj_swapped)
    (fc1_w, fc2_w), hidden_seqs = together((fc1_w, fc2_w), hidden_seqs)
    up_pair = rank_columns(fc1_w, up_offsets)

    cuts = [0]
    for item in (qv_b, proj_b, fc1_b, fc2_b):
        cuts.append(cuts[-1] + item.shape[1])
    qv_full, projb_full, upb_full, downb_full = (
        small[:, :, cuts[i] : cuts[i + 1]].transpose(1, 0, 2).reshape(2, -1).astype(F32) for i in range(4)
    )

    def at_rank(pieces):
        return pick(yi, pick(xi, *pieces[0]), pick(xi, *pieces[1]))

    def rank_vector(value, offsets):
        return at_rank(
            [
                [jnp.concatenate([value[:, at : at + size] for at, size in offsets(y, x)], 1) for x in range(2)]
                for y in range(2)
            ]
        )

    qv_rank = rank_vector(qv_full, lambda y, x: qkv_offsets(y, x)[:2])
    qkv_bias = jnp.concatenate(
        [qv_rank[:, :rank_cols], jnp.zeros((2, rank_cols), F32), qv_rank[:, rank_cols:]], 1
    )
    up_bias = rank_vector(upb_full, up_offsets)

    proj_gathered = lax.all_gather(proj_held, ("z", "c"), axis=0).reshape(shards, 2, 2, 2, rows, width)
    def two_streams(value, weights, equation):
        return [
            jnp.einsum(equation, value[:, cut], weights[j], preferred_element_type=F32)
            for j, cut in enumerate(streams)
        ]

    halves = jnp.split(fc2_w, 2, axis=1)
    down_sent = swap(pick(ci, halves[1], halves[0]), "c")
    qkv_seqs, mixed_seqs, lse_seqs = [], [], []
    for value in hidden_seqs:
        if mixed_seqs:
            value, mixed_seqs = together(value, mixed_seqs)
        pair = [
            (item + qkv_bias[j]).astype(BF)
            for j, item in enumerate(two_streams(value, qkv_rank, "btd,de->bte"))
        ]
        if not mixed_seqs:
            up_pair, pair = together(up_pair, pair)
            up_held = by_owner(*up_pair)
        mixed, lse = attend_forward(*pair)
        qkv_seqs.append(pair)
        mixed_seqs.append(mixed)
        lse_seqs.append(lse)
    down_held = jnp.where(ci == xi, pick(ci, halves[0], halves[1]), down_sent)

    def gather_up(piece):
        return natural_rows(lax.all_gather(piece, ("z", "c"), axis=0))

    def gather_down(piece):
        return lax.all_gather(piece, ("z", "c"), axis=0, tiled=True)

    up_img = gather_up(up_held[0])
    down_img = gather_down(down_held[0])
    attn = jnp.concatenate(
        exchange_square(mixed_seqs[0][:2], mixed_seqs[0][2:], mixed_seqs[1][:2], mixed_seqs[1][2:]), -1
    )
    up_rank = [up_img, gather_up(up_held[1])]
    rank = 2 * yi + xi
    relative = (0, 2, 1, 3)
    proj_rel = [
        jnp.concatenate(
            [
                lax.dynamic_index_in_dim(proj_gathered, rank ^ flip, 0, keepdims=False)[:, j]
                .transpose(1, 0, 2, 3)
                .reshape(rank_cols, width)
                for flip in relative
            ],
            0,
        )
        for j in range(2)
    ]
    out = jnp.concatenate(two_streams(attn, proj_rel, "btd,de->bte"), 1) + with_bias(projb_full)
    after = tokens + vector(2) * out

    offset_two, spread_two = statistics(after)
    normed_two = offset_two * spread_two
    hidden_two = (normed_two * (1.0 + vector(4)) + vector(3)).astype(BF)
    (silu_cond, cotangents, ct_from_x, ct_corner), hidden_two = together(
        (silu_cond, cotangents, ct_from_x, ct_corner), hidden_two
    )
    silu_all = spread(silu_cond, ("x",)).reshape(4 * shards, width)
    grad_y = cotangents.astype(F32) * live

    def gated(gate, blocks):
        return (jnp.where(stream_of_row, gate[1], gate[0]) * jnp.concatenate(blocks, 0).astype(F32)).astype(BF)

    grad_mlp_seqs = [
        gated(gate_live, (cotangents, ct_from_y)),
        gated(gate_other, (ct_from_x, *ct_corner)),
    ]
    grad_mlp = grad_mlp_seqs[0][:2]
    down_rank = [down_img, gather_down(down_held[1])]
    hidden_two_seqs = gather_square(hidden_two)
    rows_all = img + txt

    def hidden_of(j, hids, tops):
        return feed_forward_hidden(hids, tops, up_rank[j], down_rank[j], up_bias[j : j + 1], streams[j])

    def output_of(j, acts, pres, filled):
        return feed_forward_output(acts, pres, up_rank[j], down_rank[j], streams[j], filled, rows_all)

    act_img_other, pre_img_other = hidden_of(0, hidden_two_seqs[1:], grad_mlp_seqs[1:])
    mlp_other, back_other = output_of(0, act_img_other, pre_img_other, ())
    act_img_own, pre_img_own = hidden_of(0, hidden_two_seqs[:1], grad_mlp_seqs[:1])
    mlp_own, back_own = output_of(0, act_img_own, pre_img_own, ())
    act_img, pre_img = [*act_img_own, *act_img_other], [*pre_img_own, *pre_img_other]
    act_txt, pre_txt = hidden_of(1, hidden_two_seqs, grad_mlp_seqs)
    (mlp_own, mlp_other), (back_own, back_other) = output_of(
        1, act_txt, pre_txt, (*mlp_own, *mlp_other, *back_own, *back_other)
    )
    (pre_img, act_txt, pre_txt), (back_own, back_other) = together((pre_img, act_txt, pre_txt), (back_own, back_other))
    back_relays = relay_square(back_other)
    back_first = swap(back_other[1:2], "x"), swap(back_own[2:3], "y")

    def replicas(value):
        return lax.psum(value, "r") if lax.axis_size("r") > 1 else value

    def two_sums(lefts, rights):
        first, second = (
            jnp.einsum("btd,bte->de", left, right, preferred_element_type=F32) for left, right in zip(lefts, rights)
        )
        return (first + second).astype(BF)

    def owner_rows(grad):
        cols = grad.shape[1]
        value = grad.reshape(shards, 2, 2, rows, cols).transpose(0, 2, 1, 3, 4).reshape(-1, cols)
        return lax.psum_scatter(value, ("z", "c"), scatter_dimension=0, tiled=True).reshape(2, rows, cols)

    cut = streams[0]
    down_grad_img = two_sums(act_img, [top[:, cut] for top in grad_mlp_seqs])
    up_grad_img = two_sums([hid[:, cut] for hid in hidden_two_seqs], pre_img)
    down_grad_txt = weight_grad(act_txt, grad_mlp_seqs, None, streams[1])
    (back_relays, back_first), (up_grad_img, down_grad_txt) = together(
        (back_relays, back_first), (up_grad_img, down_grad_txt)
    )
    pre_txt, back_relays = together(pre_txt, back_relays)
    back_last = swap(plus(back_other[:1], back_relays[0]), "x"), swap(plus(back_own[3:4], back_relays[1]), "y")
    up_grad_txt = weight_grad(hidden_two_seqs, pre_txt, streams[1], None)
    back_last, up_grad_txt = together(back_last, up_grad_txt)
    grad_hidden_two = sum_square(back_own, (back_last[0], back_first[0]), (back_first[1], back_last[1]))
    grad_up = [owner_rows(up_grad_img), owner_rows(up_grad_txt)]
    grad_down = [
        lax.psum_scatter(down, ("z", "c"), scatter_dimension=0, tiled=True)
        for down in (down_grad_img, down_grad_txt)
    ]
    grad_after = grad_y + back_normalize(grad_hidden_two * (1.0 + vector(4)), normed_two, spread_two)
    grad_out = (vector(2) * grad_after).astype(BF)

    grad_attn = jnp.concatenate(
        [item.astype(BF) for item in two_streams(grad_out, proj_rel, "bte,de->btd")], 1
    )
    attn_late, grad_attn = together(attn, grad_attn)
    pieces = [grad_attn[:, :, i * rank_cols : (i + 1) * rank_cols] for i in range(4)]
    back = exchange_square(*pieces)
    grad_mixed_seqs = [jnp.concatenate(back[:2], 0), jnp.concatenate(back[2:], 0)]

    def hidden_back(grad_pair):
        return jnp.concatenate(
            [
                jnp.einsum("bte,de->btd", grad_pair[j], qkv_rank[j], preferred_element_type=F32).astype(BF)
                for j in range(2)
            ],
            1,
        )

    (mlp_own, mlp_other), grad_mixed_seqs = together((mlp_own, mlp_other), grad_mixed_seqs)
    mlp_first = relay_square(mlp_other), swap(mlp_other[1:2], "x"), swap(mlp_own[2:3], "y")
    grad_pair_other = attend_backward(*qkv_seqs[1], lse_seqs[1], grad_mixed_seqs[1])
    mlp_first, grad_pair_other = together(mlp_first, grad_pair_other)
    mlp_relays, mlp_x1, mlp_y2 = mlp_first
    hidden_back_other = hidden_back(grad_pair_other)
    mlp_x0 = swap(plus(mlp_other[:1], mlp_relays[0]), "x")
    mlp_y3 = swap(plus(mlp_own[3:4], mlp_relays[1]), "y")

    grad_late, hidden_back_other = together(grad_out, hidden_back_other)
    position = lax.select_n(
        rank ^ jnp.arange(4), *(jnp.full((4,), place, jnp.int32) for place in (0, 2, 1, 3))
    )

    def proj_rows(core):
        blocks = [attn_late[:, :, at * rows : (at + 1) * rows] for at in range(16)]
        left = jnp.concatenate([pick(core, blocks[at], blocks[at + 1]) for at in range(0, 16, 2)], -1)
        return [
            jnp.einsum("btd,bte->de", left[:, cut], grad_late[:, cut], preferred_element_type=F32)
            .astype(BF)
            .reshape(4, 2, rows, width)
            for cut in streams
        ]

    proj_sent, proj_kept = jnp.stack(proj_rows(1 - ci)), jnp.stack(proj_rows(ci))
    proj_received = swap(proj_sent, "c")

    hidden_relays = relay_square(hidden_back_other)
    grad_mixed_own, (hidden_back_other, proj_kept) = together(grad_mixed_seqs[0], (hidden_back_other, proj_kept))
    grad_pair_own = attend_backward(*qkv_seqs[0], lse_seqs[0], grad_mixed_own)
    (hidden_relays, mlp_x0, mlp_y3), grad_pair_own = together((hidden_relays, mlp_x0, mlp_y3), grad_pair_own)
    hidden_back_own = hidden_back(grad_pair_own)
    grad_pairs, hidden_back_own = together([grad_pair_own, grad_pair_other], hidden_back_own)
    hidden_first = swap(hidden_back_other[1:2], "x"), swap(hidden_back_own[2:3], "y")
    hidden_last = (
        swap(plus(hidden_back_other[:1], hidden_relays[0]), "x"),
        swap(plus(hidden_back_own[3:4], hidden_relays[1]), "y"),
    )

    def qkv_grad(j, pairs):
        return two_sums([hid[:, streams[j]] for hid in hidden_seqs], [pair[j] for pair in pairs])

    qkv_grad_img = qkv_grad(0, grad_pairs)
    hidden_first, qkv_grad_img = together(hidden_first, qkv_grad_img)
    (grad_pairs, proj_received), hidden_first = together((grad_pairs, proj_received), hidden_first)
    grad_proj = plus(proj_kept, proj_received)
    grad_proj = jnp.concatenate([lax.dynamic_slice_in_dim(grad_proj, position[t], 1, 1) for t in range(4)], 1)
    proj_kept, proj_received = split_swap(grad_proj, 2, yi, "y")
    qkv_grad_txt = qkv_grad(1, grad_pairs)
    grad_qkv = jnp.stack([qkv_grad_img, qkv_grad_txt])
    cols = grad_qkv.shape[2]
    grad_qkv = grad_qkv.reshape(2, shards, 2, 2, rows, cols).transpose(1, 3, 0, 2, 4, 5)
    grad_qkv = grad_qkv.reshape(2 * shards, 2, 2, rows, cols)
    hidden_last, (grad_qkv, proj_kept) = together(hidden_last, (grad_qkv, proj_kept))
    grad_hidden = sum_square(
        hidden_back_own, (hidden_last[0], hidden_first[0]), (hidden_first[1], hidden_last[1])
    )
    grad_qkv = lax.psum_scatter(grad_qkv, ("z", "c"), scatter_dimension=0, tiled=True).reshape(2, 2, rows, cols)

    (mlp_own, grad_pairs, grad_up, grad_down), grad_hidden = together(
        (mlp_own, grad_pairs, grad_up, grad_down), grad_hidden
    )
    mlp = sum_square(mlp_own, (mlp_x0, mlp_x1), (mlp_y2, mlp_y3)) + with_bias(downb_full)
    result = ((after + vector(5) * mlp) * live).astype(BF)
    up_pair = split_swap(replicas(jnp.stack(grad_up)), 1, yi, "y")
    down = replicas(jnp.stack(grad_down))
    down_other = swap(down, "x")
    grad_hidden_late, (up_kept, down) = together(grad_hidden, (up_pair[0], down))
    up_pair = up_kept, up_pair[1]

    grad_tokens = grad_after + back_normalize(grad_hidden * (1.0 + vector(1)), normed, spread_one)

    def from_slot(value):
        return paired(ci, value[:1], swap(value[1:], "c"), 0)

    result = from_slot(result)
    grad_tokens = from_slot(grad_tokens)

    def token_sums(value):
        return jnp.stack([jnp.sum(value[:, cut], axis=(0, 1)) for cut in streams])

    sums = jnp.stack(
        [
            token_sums(grad_hidden_late),
            token_sums(grad_hidden_late * normed),
            token_sums(out * grad_after),
            token_sums(grad_hidden_two),
            token_sums(grad_hidden_two * normed_two),
            token_sums(mlp * grad_y),
        ],
        1,
    ).reshape(2, 6 * width)
    up_pair, sums = together(up_pair, sums)
    up_mine = jnp.concatenate(up_pair, 1)
    dmod = (sums + swap(sums, "y")).astype(BF)
    (late_pre, late_out, late_mlp, proj_received), dmod = together(
        ((pre_img, pre_txt), grad_out, grad_mlp, proj_received), dmod
    )
    proj_kept, proj_received = split_swap(plus(proj_kept, proj_received), 0, xi, "x")
    dmod_rep = spread(dmod, ("z", "c"))
    qkv_pair = split_swap(replicas(grad_qkv), 1, yi, "y")
    (dmod_rep, proj_kept), qkv_kept = together((dmod_rep, proj_kept), qkv_pair[0])
    qkv_pair = qkv_kept, qkv_pair[1]
    grad_proj = plus(proj_kept, proj_received).reshape(shards * rows, width)
    grad_proj = replicas(lax.psum_scatter(grad_proj, "z", scatter_dimension=0, tiled=True))
    g_proj_w = paired(xi, grad_proj[None], swap(grad_proj, "x")[None], 0).astype(F32)
    blocks = (pick(xi, down, down_other), pick(xi, down_other, down))
    g_fc2_w = paired(ci, pick(ci, *blocks), swap(pick(ci, blocks[1], blocks[0]), "c"), 1).astype(F32)
    qkv_mine = jnp.concatenate(qkv_pair, 1)
    g_qkv_w = owner_columns(qkv_mine, swap(qkv_mine, "x"), xi, yi, 3)
    dsilu_part = jnp.einsum("sjm,jdm->sd", dmod_rep, ada_w, preferred_element_type=F32)
    dsilu = spread(dsilu_part, ("z", "y", "c")).transpose(1, 0, 2).reshape(2 * shards, owners * rows)
    gate = jax.nn.sigmoid(cond_value)
    d_cond = dsilu * gate * (1.0 + cond_value * (1.0 - gate))
    dmod_all = spread(dmod_rep, ("x",)).reshape(4 * shards, 2, 6 * width)
    if lax.axis_size("r") > 1:
        dmod_all = lax.all_gather(dmod_all, "r", axis=0, tiled=True)
        silu_all = lax.all_gather(silu_all, "r", axis=0, tiled=True)
    silu_cols = lax.dynamic_slice_in_dim(silu_all, owner * rows, rows, 1)
    g_ada_w = jnp.einsum("sd,sjm->jdm", silu_cols, dmod_all, preferred_element_type=F32)
    g_ada_b = jnp.sum(
        lax.dynamic_slice_in_dim(dmod_all, owner * ada_b.shape[1], ada_b.shape[1], 2).astype(F32), axis=0
    )

    here = ((jnp.arange(2)[:, None] == yi) & (jnp.arange(2)[None] == xi)).astype(F32)
    qkv_sums = jnp.stack(
        [sum(jnp.sum(pair[j].astype(F32), axis=(0, 1)) for pair in grad_pairs) for j in range(2)]
    ).reshape(2, 3, rank_cols)
    qv_sums = jnp.stack([qkv_sums[:, 0], qkv_sums[:, 2]], 1)
    qv_placed = (qv_sums[:, :, None, None] * here[:, :, None]).reshape(2, 2 * width)
    up_sums = jnp.stack(
        [sum(jnp.sum(pre.astype(F32), axis=(0, 1)) for pre in late_pre[j]) for j in range(2)]
    ).reshape(2, shards, ff_block)
    up_placed = (up_sums[:, :, None, None] * here[:, :, None]).reshape(2, owners * ff_block)
    biases = jnp.concatenate(
        [qv_placed, token_sums(late_out.astype(F32)), up_placed, token_sums(late_mlp.astype(F32))], 1
    )
    biases = replicas(total(biases, ("c", "y", "z", "x")))
    up_mine, biases = together(up_mine, biases)
    g_fc1_w = owner_columns(up_mine, swap(up_mine, "x"), xi, yi, shards)
    g_biases = []
    start = 0
    for item in (qv_b, proj_b, fc1_b, fc2_b):
        cols = item.shape[1]
        g_biases.append(lax.dynamic_slice_in_dim(biases, start + owner * cols, cols, 1))
        start += owners * cols
    return (
        result[:, :img],
        result[:, img:],
        grad_tokens[:, :img],
        grad_tokens[:, img:],
        d_cond,
        g_ada_w,
        g_ada_b,
        g_qkv_w,
        g_biases[0],
        g_proj_w,
        g_biases[1],
        g_fc1_w,
        g_biases[2],
        g_fc2_w,
        g_biases[3],
    )


def solution(mesh):
    reps, shards, seqs = mesh.shape["rep"], mesh.shape["shard"], mesh.shape["seq"]
    fine = Mesh(mesh.devices.reshape(reps // 2, 2, shards, seqs // 2, 2), ("r", "x", "z", "y", "c"))
    group = ("r", "x", "z")
    token = P(group, ("y", "c"), None)
    cond = P(("r", "x"), None)
    matrix = P(None, ("z", "y", "c"), None)
    vector = P(None, ("z", "y", "c"))
    return jax.shard_map(
        on_device,
        mesh=fine,
        in_specs=(token, token, cond, P(group), token, token) + (matrix, vector) * 5,
        out_specs=(token, token, token, token, cond) + (matrix, vector) * 5,
        check_vma=False,
    )
```

```python
import jax
import jax.numpy as jnp
from jax import lax
from jax.experimental import pallas as pl
from jax.experimental.pallas import tpu as pltpu
from jax.sharding import Mesh, PartitionSpec as P

HD = 64
LOG2E = 1.4426950408889634
BF = jnp.bfloat16
F32 = jnp.float32
FLIP = ((0, 1), (1, 0))


def matmul(left, right, left_dim, right_dim):
    return lax.dot_general(
        left, right, (((left_dim,), (right_dim,)), ((), ())), preferred_element_type=F32
    )


def join_streams(img_ref, txt_ref, cut):
    img = img_ref[:, :, cut]
    txt = txt_ref[:, :, cut]
    return jnp.concatenate([img.reshape(-1, HD), txt.reshape(-1, HD)], 0)


def attend_forward_kernel(img_ref, txt_ref, out_ref, lse_ref, *, heads, scale):
    blocks = img_ref.shape[0]
    width = heads * HD
    rows = out_ref.shape[1]
    for head in range(heads):
        cut = slice(head * HD, head * HD + HD)
        keys = join_streams(img_ref, txt_ref, slice(width + cut.start, width + cut.stop))
        values_t = join_streams(img_ref, txt_ref, slice(2 * width + cut.start, 2 * width + cut.stop)).T
        for block in range(blocks):
            queries = jnp.concatenate([img_ref[block, :, cut], txt_ref[block, :, cut]], 0)
            raw = matmul(keys, queries, 1, 1) * scale
            top = jnp.max(raw, axis=0, keepdims=True)
            grown = jnp.exp2(raw - top)
            total = jnp.sum(grown, axis=0, keepdims=True)
            mixed_t = matmul(values_t, grown.astype(BF), 1, 0) * (1.0 / total)
            out_ref[block, :, cut] = mixed_t.T.astype(BF)
            lse_ref[head : head + 1, block * rows : (block + 1) * rows] = top + jnp.log2(total)


def attend_backward_kernel(
    img_ref, txt_ref, lse_ref, grad_ref, img_out, txt_out, sums_out, key_sum, value_sum, *, heads, scale
):
    blocks, img_rows = img_ref.shape[:2]
    txt_rows = txt_ref.shape[1]
    width = heads * HD
    rows = grad_ref.shape[1]
    for head in range(heads):
        cut = slice(head * HD, head * HD + HD)
        key_cut = slice(width + cut.start, width + cut.stop)
        value_cut = slice(2 * width + cut.start, 2 * width + cut.stop)
        keys = join_streams(img_ref, txt_ref, key_cut)
        values = join_streams(img_ref, txt_ref, value_cut)
        keys_t = keys.T
        query_sums = [0.0, 0.0]
        for block in range(blocks):
            queries = jnp.concatenate([img_ref[block, :, cut], txt_ref[block, :, cut]], 0)
            grad = grad_ref[block, :, cut]
            raw = matmul(keys, queries, 1, 1)
            prob = jnp.exp2(raw * scale - lse_ref[head : head + 1, block * rows : (block + 1) * rows])
            value_part = matmul(prob.astype(BF), grad, 1, 0)
            grad_prob = matmul(values, grad, 1, 1)
            delta = jnp.sum(prob * grad_prob, axis=0, keepdims=True)
            grad_raw = (prob * (grad_prob - delta)).astype(BF)
            key_part = matmul(grad_raw, queries, 1, 0)
            if block == 0:
                value_sum[...] = value_part
                key_sum[...] = key_part
            else:
                value_sum[...] += value_part
                key_sum[...] += key_part
            grad_query = (matmul(keys_t, grad_raw, 1, 0) * HD**-0.5).T.astype(BF)
            img_out[block, :, cut] = grad_query[:img_rows]
            txt_out[block, :, cut] = grad_query[img_rows:]
            grad_query = grad_query.astype(F32)
            query_sums[0] += jnp.sum(grad_query[:img_rows], axis=0, keepdims=True)
            query_sums[1] += jnp.sum(grad_query[img_rows:], axis=0, keepdims=True)
        rounded = value_sum[...].astype(BF).astype(F32)
        value_sums = (
            jnp.sum(rounded[: blocks * img_rows], axis=0, keepdims=True),
            jnp.sum(rounded[blocks * img_rows :], axis=0, keepdims=True),
        )
        for stream in range(2):
            sums_out[stream : stream + 1, cut] = query_sums[stream]
            sums_out[stream : stream + 1, key_cut] = jnp.zeros((1, HD), F32)
            sums_out[stream : stream + 1, value_cut] = value_sums[stream]
        for there, total, factor in ((key_cut, key_sum, HD**-0.5), (value_cut, value_sum, 1.0)):
            for block in range(blocks):
                img_out[block, :, there] = (total[block * img_rows : (block + 1) * img_rows] * factor).astype(BF)
                at = blocks * img_rows + block * txt_rows
                txt_out[block, :, there] = (total[at : at + txt_rows] * factor).astype(BF)


def whole(shape):
    return pl.BlockSpec(shape, lambda: (0,) * len(shape))


def attend_cost(img, txt, heads, products):
    length = img.shape[0] * (img.shape[1] + txt.shape[1])
    return pl.CostEstimate(
        flops=products * 18 * heads * length * length * HD,
        bytes_accessed=4 * (img.size + txt.size),
        transcendentals=heads * length * length,
    )


def attend_forward(img, txt):
    blocks = img.shape[0]
    rows = img.shape[1] + txt.shape[1]
    heads = img.shape[2] // (3 * HD)
    outs = ((blocks, rows, heads * HD), (heads, blocks * rows))
    return pl.pallas_call(
        lambda *refs: attend_forward_kernel(*refs, heads=heads, scale=HD**-0.5 * LOG2E),
        in_specs=[whole(img.shape), whole(txt.shape)],
        out_specs=[whole(shape) for shape in outs],
        out_shape=[jax.ShapeDtypeStruct(outs[0], BF), jax.ShapeDtypeStruct(outs[1], F32)],
        compiler_params=pltpu.CompilerParams(vmem_limit_bytes=40 << 20),
        cost_estimate=attend_cost(img, txt, heads, 2),
        name="attend_forward",
    )(img, txt)


def attend_backward(img, txt, lse, grad):
    heads = img.shape[2] // (3 * HD)
    length = img.shape[0] * (img.shape[1] + txt.shape[1])
    return pl.pallas_call(
        lambda *refs: attend_backward_kernel(*refs, heads=heads, scale=HD**-0.5 * LOG2E),
        in_specs=[whole(value.shape) for value in (img, txt, lse, grad)],
        out_specs=[whole(img.shape), whole(txt.shape), whole((2, img.shape[2]))],
        out_shape=[
            jax.ShapeDtypeStruct(img.shape, BF),
            jax.ShapeDtypeStruct(txt.shape, BF),
            jax.ShapeDtypeStruct((2, img.shape[2]), F32),
        ],
        scratch_shapes=[pltpu.VMEM((length, HD), F32), pltpu.VMEM((length, HD), F32)],
        compiler_params=pltpu.CompilerParams(vmem_limit_bytes=40 << 20),
        cost_estimate=attend_cost(img, txt, heads, 5),
        name="attend_backward",
    )(img, txt, lse, grad)


CURVE = 0.7978845608028654
CUBIC = 0.044715


def gelu_and_slope(value):
    square = value * value
    bend = jnp.tanh(CURVE * value * (1.0 + CUBIC * square))
    rise = 0.5 + 0.5 * bend
    slope = rise + 0.5 * CURVE * value * (1.0 - bend * bend) * (1.0 + 3.0 * CUBIC * square)
    return value * rise, slope


def rows_of(refs):
    values = [ref[...].reshape(-1, ref.shape[2]) for ref in refs]
    return values[0] if len(values) == 1 else jnp.concatenate(values, 0)


def store_rows(refs, value):
    start = 0
    for ref in refs:
        stop = start + ref.shape[0] * ref.shape[1]
        ref[...] = value[start:stop].reshape(ref.shape)
        start = stop


def hidden_kernel(*refs, count):
    hids, tops, (up_ref, down_ref, bias_ref) = refs[:count], refs[count : 2 * count], refs[2 * count : 2 * count + 3]
    acts, grads, sums_ref = refs[2 * count + 3 : 3 * count + 3], refs[3 * count + 3 : -1], refs[-1]
    pre = matmul(rows_of(hids), up_ref[...], 1, 0) + bias_ref[...]
    grad_act = matmul(rows_of(tops), down_ref[...], 1, 1)
    act, slope = gelu_and_slope(pre)
    store_rows(acts, act.astype(BF))
    grad_pre = (grad_act * slope).astype(BF)
    store_rows(grads, grad_pre)
    sums_ref[...] = jnp.sum(grad_pre.astype(F32), axis=0, keepdims=True)


def output_kernel(*refs, count):
    acts, grads, (up_ref, down_ref) = refs[:count], refs[count : 2 * count], refs[2 * count : 2 * count + 2]
    mlps, backs = refs[-2 * count : -count], refs[-count:]
    store_rows(backs, matmul(rows_of(grads), up_ref[...], 1, 1).astype(BF))
    store_rows(mlps, matmul(rows_of(acts), down_ref[...], 1, 0).astype(BF))


def feed_forward_hidden(hids, tops, up, down, bias, cut):
    count = len(hids)
    blocks, _, width = hids[0].shape
    rows = cut.stop - cut.start
    ff = up.shape[1]
    tile = 256 if ff % 256 == 0 else ff
    token = pl.BlockSpec((blocks, rows, width), lambda f: (0, cut.start // rows, 0))
    out_spec = pl.BlockSpec((blocks, rows, tile), lambda f: (0, 0, f))
    size = count * blocks * rows
    outs = pl.pallas_call(
        lambda *refs: hidden_kernel(*refs, count=count),
        grid=(ff // tile,),
        in_specs=[
            *[token] * (2 * count),
            pl.BlockSpec((width, tile), lambda f: (0, f)),
            pl.BlockSpec((tile, width), lambda f: (f, 0)),
            pl.BlockSpec((1, tile), lambda f: (0, f)),
        ],
        out_specs=[*[out_spec] * (2 * count), pl.BlockSpec((1, tile), lambda f: (0, f))],
        out_shape=[
            *[jax.ShapeDtypeStruct((blocks, rows, ff), BF)] * (2 * count),
            jax.ShapeDtypeStruct((1, ff), F32),
        ],
        compiler_params=pltpu.CompilerParams(vmem_limit_bytes=48 << 20),
        cost_estimate=pl.CostEstimate(
            flops=8 * size * width * ff, bytes_accessed=4 * size * (width + ff) + 4 * up.size, transcendentals=size * ff
        ),
        name="feed_forward_hidden",
    )(*hids, *tops, up, down, bias)
    return outs[:count], outs[count : 2 * count], outs[-1]


def feed_forward_output(acts, grads, up, down, cut, filled, all_rows):
    count = len(acts)
    blocks, rows, ff = acts[0].shape
    width = up.shape[0]
    tile = 256 if width % 256 == 0 else width
    token = pl.BlockSpec((blocks, rows, ff), lambda n: (0, 0, 0))
    out_spec = pl.BlockSpec((blocks, rows, tile), lambda n: (0, cut.start // rows, n))
    size = count * blocks * rows
    outs = pl.pallas_call(
        lambda *refs: output_kernel(*refs, count=count),
        grid=(width // tile,),
        in_specs=[
            *[token] * (2 * count),
            pl.BlockSpec((tile, ff), lambda n: (n, 0)),
            pl.BlockSpec((ff, tile), lambda n: (0, n)),
            *(pl.BlockSpec(memory_space=pl.ANY) for _ in filled),
        ],
        out_specs=[out_spec] * (2 * count),
        out_shape=[jax.ShapeDtypeStruct((blocks, all_rows, width), BF)] * (2 * count),
        input_output_aliases={2 * count + 2 + at: at for at in range(len(filled))},
        compiler_params=pltpu.CompilerParams(vmem_limit_bytes=48 << 20),
        cost_estimate=pl.CostEstimate(
            flops=8 * size * width * ff, bytes_accessed=4 * size * (width + ff) + 4 * up.size, transcendentals=0
        ),
        name="feed_forward_output",
    )(*acts, *grads, up, down, *filled)
    return outs[:count], outs[count:]


def weight_grad_kernel(*refs, count):
    lefts, rights, out_ref, turned = refs[:count], refs[count : 2 * count], refs[2 * count], refs[2 * count + 1]
    rows = lefts[0].shape[0] * lefts[0].shape[1]

    @pl.when(pl.program_id(0) == 0)
    def _():
        for at, left in enumerate(lefts):
            turned[:, at * rows : (at + 1) * rows] = left[...].reshape(rows, left.shape[2]).T

    total = matmul(turned[:, :rows], rights[0][...].reshape(rows, -1), 1, 0)
    for at in range(1, count):
        total = total + matmul(turned[:, at * rows : (at + 1) * rows], rights[at][...].reshape(rows, -1), 1, 0)
    out_ref[...] = total.astype(BF)


def weight_grad(lefts, rights, left_cut, right_cut):
    count = len(lefts)

    def rows_and_place(value, cut):
        rows = value.shape[1] if cut is None else cut.stop - cut.start
        return rows, 0 if cut is None else cut.start // rows

    blocks, _, left_cols = lefts[0].shape
    right_cols = rights[0].shape[2]
    rows, left_at = rows_and_place(lefts[0], left_cut)
    _, right_at = rows_and_place(rights[0], right_cut)
    tile = next(tile for tile in (512, 384, right_cols) if right_cols % tile == 0)
    tokens = count * blocks * rows
    return pl.pallas_call(
        lambda *refs: weight_grad_kernel(*refs, count=count),
        grid=(right_cols // tile,),
        in_specs=[
            *[pl.BlockSpec((blocks, rows, left_cols), lambda n: (0, left_at, 0))] * count,
            *[pl.BlockSpec((blocks, rows, tile), lambda n: (0, right_at, n))] * count,
        ],
        out_specs=pl.BlockSpec((left_cols, tile), lambda n: (0, n)),
        out_shape=jax.ShapeDtypeStruct((left_cols, right_cols), BF),
        scratch_shapes=[pltpu.VMEM((left_cols, tokens), BF)],
        compiler_params=pltpu.CompilerParams(vmem_limit_bytes=48 << 20),
        cost_estimate=pl.CostEstimate(
            flops=3 * tokens * left_cols * right_cols,
            bytes_accessed=2 * tokens * (left_cols + right_cols) + 2 * left_cols * right_cols,
            transcendentals=0,
        ),
        name="weight_grad",
    )(*lefts, *rights)


def owner_kernel(place_ref, mine_ref, others_ref, out_ref):
    block = mine_ref.shape[3]
    for rank in range(4):
        y = (rank // 2 + place_ref[1]) % 2
        piece = jnp.where(rank % 2 == place_ref[0], mine_ref[:, y], others_ref[:, y])
        out_ref[:, :, rank * block : (rank + 1) * block] = piece.astype(F32)


def owner_columns(mine, others, xi, yi, parts):
    streams, _, rows, cols = mine.shape
    block = cols // parts
    place = jnp.stack([xi, yi]).astype(jnp.int32)
    spec = pl.BlockSpec((streams, 2, rows, block), lambda part, place: (0, 0, 0, part))
    return pl.pallas_call(
        owner_kernel,
        grid_spec=pltpu.PrefetchScalarGridSpec(
            num_scalar_prefetch=1,
            grid=(parts,),
            in_specs=[spec, spec],
            out_specs=pl.BlockSpec((streams, rows, 4 * block), lambda part, place: (0, 0, part)),
        ),
        out_shape=jax.ShapeDtypeStruct((streams, rows, 4 * cols), F32),
        compiler_params=pltpu.CompilerParams(vmem_limit_bytes=32 << 20),
        cost_estimate=pl.CostEstimate(flops=0, bytes_accessed=24 * mine.size, transcendentals=0),
        name="owner_columns",
    )(place, mine, others)


def swap(value, axis):
    return lax.ppermute(value, axis, FLIP)


def shift_xor(value, axis, bit):
    return lax.ppermute(value, axis, [(i, i ^ bit) for i in range(lax.axis_size(axis))])


def shift(value, axis, step):
    size = lax.axis_size(axis)
    return lax.ppermute(value, axis, [(i, (i + step) % size) for i in range(size)])


def swap_both(value):
    return lax.ppermute(value, ("x", "y"), [(i, 3 - i) for i in range(4)])


def pick(index, first, second):
    return jnp.where(index == 0, first, second)


def paired(index, own, other, axis):
    return jnp.where(
        index == 0, jnp.concatenate([own, other], axis), jnp.concatenate([other, own], axis)
    )


def split_swap(value, dim, index, axis):
    first, second = jnp.split(value, 2, axis=dim)
    return pick(index, first, second), swap(pick(index, second, first), axis)


def spread(value, axes):
    value = value[None]
    for axis in reversed(axes):
        size, here = lax.axis_size(axis), lax.axis_index(axis)
        bit = 1
        while bit < size:
            value = paired((here // bit) % 2, value, shift_xor(value, axis, bit), 0)
            bit *= 2
    return value


def total(value, axes):
    for axis in axes:
        bit = 1
        while bit < lax.axis_size(axis):
            value = value + shift_xor(value, axis, bit)
            bit *= 2
    return value


def together(values, others):
    return lax.optimization_barrier((values, others))


def gather_square(own):
    from_x, from_y = swap(own, "x"), swap(own, "y")
    corner_a, corner_b = swap(from_x[:1], "y"), swap(from_y[1:], "x")
    return jnp.concatenate([own, from_y], 0), jnp.concatenate([from_x, corner_a, corner_b], 0)


def plus(first, second):
    return (first.astype(F32) + second.astype(F32)).astype(BF)


def relay_square(other):
    return swap(other[2:3], "y"), swap(other[3:4], "x")


def send_x(other, relays):
    return swap(plus(other[:1], relays[0]), "x"), swap(other[1:2], "x")


def send_y(own, relays):
    return swap(own[2:3], "y"), swap(plus(own[3:4], relays[1]), "y")


def sum_square(own, from_x, from_y):
    return own[:2].astype(F32) + jnp.concatenate(from_x, 0).astype(F32) + jnp.concatenate(from_y, 0).astype(F32)


def exchange_square(own, for_y, for_x, for_corner):
    return [own, swap(for_y, "y"), swap(for_x, "x"), swap_both(for_corner)]


def on_device(
    x_img,
    x_txt,
    cond,
    counts,
    ct_img,
    ct_txt,
    ada_w,
    ada_b,
    qkv_w,
    qv_b,
    proj_w,
    proj_b,
    fc1_w,
    fc1_b,
    fc2_w,
    fc2_b,
):
    xi, yi, zi, ci = (lax.axis_index(name) for name in ("x", "y", "z", "c"))
    shards = lax.axis_size("z")
    owners = 4 * shards
    owner = zi * 4 + yi * 2 + ci
    width = x_img.shape[2]
    rows = ada_w.shape[1]
    rank_cols = width // 4
    ff_block = fc2_w.shape[1]
    img = x_img.shape[1]
    txt = x_txt.shape[1]
    live = (ci < counts[0]).astype(F32)
    streams = (slice(0, img), slice(img, img + txt))

    def to_slot(img_part, txt_part):
        both = jnp.concatenate([img_part, txt_part], 1)
        kept, received = split_swap(both, 0, ci, "c")
        return jnp.concatenate([kept, received], 0)

    tokens = to_slot(x_img, x_txt).astype(F32)

    cotangents = to_slot(ct_img, ct_txt)
    ct_from_x, ct_from_y = swap(cotangents, "x"), swap(cotangents, "y")

    cond_value = cond.astype(F32)
    silu_cond = jax.nn.silu(cond_value).astype(BF)
    silu_own = lax.dynamic_slice_in_dim(silu_cond, owner * rows, rows, 1).reshape(shards, 2, rows)
    bias_full = lax.dynamic_update_slice_in_dim(
        jnp.zeros((2, 6 * width), F32), ada_b.astype(F32), owner * ada_b.shape[1], 1
    )

    def partial_mod(slots):
        return jnp.einsum("sd,jdm->sjm", slots, ada_w, preferred_element_type=F32) + bias_full

    mod_peer = partial_mod(pick(ci, silu_own[:, 1], silu_own[:, 0]))
    mod_sent = swap(mod_peer, "c")
    mod_own = partial_mod(pick(ci, silu_own[:, 0], silu_own[:, 1]))
    mod = mod_own + mod_sent
    small = spread(jnp.concatenate([qv_b, proj_b, fc1_b, fc2_b], 1), ("z", "c", "y"))
    small, mod = together(small, mod)
    small = small.reshape(shards, 2, 2, 2, -1).swapaxes(1, 2).reshape(owners, 2, -1)
    mod_here = lax.dynamic_index_in_dim(mod, zi, 0, keepdims=False)
    for step in range(1, shards):
        there = lax.dynamic_index_in_dim(mod, (zi + step) % shards, 0, keepdims=False)
        mod_here = mod_here + shift(there, "z", step)
    mod = (mod_here + swap(mod_here, "y")).reshape(2, 6, width)
    stream_of_row = (jnp.arange(img + txt) >= img)[None, :, None]

    def vector(index):
        return jnp.where(stream_of_row, mod[1, index], mod[0, index])

    def with_bias(pair):
        return jnp.where(stream_of_row, pair[1], pair[0])

    def rank_columns(weight, offsets):
        by_y = [
            pick(
                xi,
                *(
                    jnp.concatenate([weight[:, :, at : at + size] for at, size in offsets(y, x)], 2)
                    for x in range(2)
                ),
            )
            for y in range(2)
        ]
        return pick(yi, by_y[0], by_y[1]), swap(pick(yi, by_y[1], by_y[0]), "y")

    def by_owner(kept, received):
        return jnp.stack([pick(yi, kept, received), pick(yi, received, kept)], 1)

    def natural_rows(gathered):
        cols = gathered.shape[3]
        return gathered.reshape(shards, 2, 2, rows, cols).transpose(0, 2, 1, 3, 4).reshape(width, cols)

    def qkv_offsets(y, x):
        return [(third * width + (2 * y + x) * rank_cols, rank_cols) for third in range(3)]

    def up_offsets(y, x):
        return [((z * 4 + y * 2 + x) * ff_block, ff_block) for z in range(shards)]

    qkv_pair = rank_columns(qkv_w, qkv_offsets)
    proj_swapped = swap(proj_w, "y")
    qkv_held = by_owner(*qkv_pair)
    qkv_gathered = lax.all_gather(qkv_held, ("z", "c"), axis=0)
    qkv_rank = [natural_rows(qkv_gathered[:, j]) for j in range(2)]

    def statistics(value):
        centre = jnp.mean(value, axis=-1, keepdims=True)
        offset = value - centre
        return offset, lax.rsqrt(jnp.mean(offset * offset, axis=-1, keepdims=True) + 1e-06)

    def back_normalize(grad, normed, scale):
        return scale * (
            grad
            - jnp.mean(grad, axis=-1, keepdims=True)
            - normed * jnp.mean(grad * normed, axis=-1, keepdims=True)
        )

    offset, spread_one = statistics(tokens)
    normed = offset * spread_one
    hidden = (normed * (1.0 + vector(1)) + vector(0)).astype(BF)
    gate_live = mod[:, 5] * live
    gate_other = swap(gate_live, "x")
    hidden_x, hidden_y = swap(hidden, "x"), swap(hidden, "y")
    (ct_from_x, ct_from_y), (hidden_x, hidden_y) = together((ct_from_x, ct_from_y), (hidden_x, hidden_y))
    hidden_corner = swap(hidden_x[:1], "y"), swap(hidden_y[1:], "x")
    ct_corner = swap(ct_from_x[:1], "y"), swap(ct_from_y[1:], "x")
    hidden_seqs = [
        jnp.concatenate([hidden, hidden_y], 0),
        jnp.concatenate([hidden_x, *hidden_corner], 0),
    ]

    proj_held = by_owner(proj_w, proj_swapped)
    (fc1_w, fc2_w), hidden_seqs = together((fc1_w, fc2_w), hidden_seqs)
    up_pair = rank_columns(fc1_w, up_offsets)

    cuts = [0]
    for item in (qv_b, proj_b, fc1_b, fc2_b):
        cuts.append(cuts[-1] + item.shape[1])
    qv_full, projb_full, upb_full, downb_full = (
        small[:, :, cuts[i] : cuts[i + 1]].transpose(1, 0, 2).reshape(2, -1).astype(F32) for i in range(4)
    )

    def at_rank(pieces):
        return pick(yi, pick(xi, *pieces[0]), pick(xi, *pieces[1]))

    def rank_vector(value, offsets):
        return at_rank(
            [
                [jnp.concatenate([value[:, at : at + size] for at, size in offsets(y, x)], 1) for x in range(2)]
                for y in range(2)
            ]
        )

    qv_rank = rank_vector(qv_full, lambda y, x: qkv_offsets(y, x)[:2])
    qkv_bias = jnp.concatenate(
        [qv_rank[:, :rank_cols], jnp.zeros((2, rank_cols), F32), qv_rank[:, rank_cols:]], 1
    )
    up_bias = rank_vector(upb_full, up_offsets)

    proj_gathered = lax.all_gather(proj_held, ("z", "c"), axis=0).reshape(shards, 2, 2, 2, rows, width)
    def two_streams(value, weights, equation):
        return [
            jnp.einsum(equation, value[:, cut], weights[j], preferred_element_type=F32)
            for j, cut in enumerate(streams)
        ]

    halves = jnp.split(fc2_w, 2, axis=1)
    down_sent = swap(pick(ci, halves[1], halves[0]), "c")
    qkv_seqs, mixed_seqs, lse_seqs = [], [], []
    for value in hidden_seqs:
        if mixed_seqs:
            value, mixed_seqs = together(value, mixed_seqs)
        pair = [
            (item + qkv_bias[j]).astype(BF)
            for j, item in enumerate(two_streams(value, qkv_rank, "btd,de->bte"))
        ]
        if not mixed_seqs:
            up_pair, pair = together(up_pair, pair)
            up_held = by_owner(*up_pair)
        mixed, lse = attend_forward(*pair)
        qkv_seqs.append(pair)
        mixed_seqs.append(mixed)
        lse_seqs.append(lse)
    down_held = jnp.where(ci == xi, pick(ci, halves[0], halves[1]), down_sent)

    def gather_up(piece):
        return natural_rows(lax.all_gather(piece, ("z", "c"), axis=0))

    def gather_down(piece):
        return lax.all_gather(piece, ("z", "c"), axis=0, tiled=True)

    up_img = gather_up(up_held[0])
    down_img = gather_down(down_held[0])
    attn = jnp.concatenate(
        exchange_square(mixed_seqs[0][:2], mixed_seqs[0][2:], mixed_seqs[1][:2], mixed_seqs[1][2:]), -1
    )
    up_rank = [up_img, gather_up(up_held[1])]
    rank = 2 * yi + xi
    relative = (0, 2, 1, 3)
    proj_rel = [
        jnp.concatenate(
            [
                lax.dynamic_index_in_dim(proj_gathered, rank ^ flip, 0, keepdims=False)[:, j]
                .transpose(1, 0, 2, 3)
                .reshape(rank_cols, width)
                for flip in relative
            ],
            0,
        )
        for j in range(2)
    ]
    out = jnp.concatenate(two_streams(attn, proj_rel, "btd,de->bte"), 1) + with_bias(projb_full)
    after = tokens + vector(2) * out

    offset_two, spread_two = statistics(after)
    normed_two = offset_two * spread_two
    hidden_two = (normed_two * (1.0 + vector(4)) + vector(3)).astype(BF)
    (silu_cond, cotangents, ct_from_x, ct_corner), hidden_two = together(
        (silu_cond, cotangents, ct_from_x, ct_corner), hidden_two
    )
    silu_all = spread(silu_cond, ("x",)).reshape(4 * shards, width)
    grad_y = cotangents.astype(F32) * live

    def gated(gate, blocks):
        return (jnp.where(stream_of_row, gate[1], gate[0]) * jnp.concatenate(blocks, 0).astype(F32)).astype(BF)

    grad_mlp_seqs = [
        gated(gate_live, (cotangents, ct_from_y)),
        gated(gate_other, (ct_from_x, *ct_corner)),
    ]
    grad_mlp = grad_mlp_seqs[0][:2]
    down_rank = [down_img, gather_down(down_held[1])]
    hidden_two_seqs = gather_square(hidden_two)
    rows_all = img + txt

    def hidden_of(j, hids, tops):
        return feed_forward_hidden(hids, tops, up_rank[j], down_rank[j], up_bias[j : j + 1], streams[j])

    def output_of(j, acts, pres, filled):
        return feed_forward_output(acts, pres, up_rank[j], down_rank[j], streams[j], filled, rows_all)

    act_img_other, pre_img_other, sums_other = hidden_of(0, hidden_two_seqs[1:], grad_mlp_seqs[1:])
    mlp_other, back_other = output_of(0, act_img_other, pre_img_other, ())
    act_img_own, pre_img_own, sums_own = hidden_of(0, hidden_two_seqs[:1], grad_mlp_seqs[:1])
    mlp_own, back_own = output_of(0, act_img_own, pre_img_own, ())
    act_img, pre_img = [*act_img_own, *act_img_other], [*pre_img_own, *pre_img_other]
    act_txt, pre_txt, sums_txt = hidden_of(1, hidden_two_seqs, grad_mlp_seqs)
    (mlp_own, mlp_other), (back_own, back_other) = output_of(
        1, act_txt, pre_txt, (*mlp_own, *mlp_other, *back_own, *back_other)
    )
    (pre_img, act_txt, pre_txt), (back_own, back_other) = together((pre_img, act_txt, pre_txt), (back_own, back_other))
    back_relays = relay_square(back_other)
    back_first = swap(back_other[1:2], "x"), swap(back_own[2:3], "y")

    def replicas(value):
        return lax.psum(value, "r") if lax.axis_size("r") > 1 else value

    def two_sums(lefts, rights):
        first, second = (
            jnp.einsum("btd,bte->de", left, right, preferred_element_type=F32) for left, right in zip(lefts, rights)
        )
        return (first + second).astype(BF)

    def owner_rows(grad):
        cols = grad.shape[1]
        value = grad.reshape(shards, 2, 2, rows, cols).transpose(0, 2, 1, 3, 4).reshape(-1, cols)
        return lax.psum_scatter(value, ("z", "c"), scatter_dimension=0, tiled=True).reshape(2, rows, cols)

    cut = streams[0]
    down_grad_img = two_sums(act_img, [top[:, cut] for top in grad_mlp_seqs])
    up_grad_img = two_sums([hid[:, cut] for hid in hidden_two_seqs], pre_img)
    down_grad_txt = weight_grad(act_txt, grad_mlp_seqs, None, streams[1])
    (back_relays, back_first), (up_grad_img, down_grad_txt) = together(
        (back_relays, back_first), (up_grad_img, down_grad_txt)
    )
    pre_txt, back_relays = together(pre_txt, back_relays)
    back_last = swap(plus(back_other[:1], back_relays[0]), "x"), swap(plus(back_own[3:4], back_relays[1]), "y")
    up_grad_txt = weight_grad(hidden_two_seqs, pre_txt, streams[1], None)
    back_last, up_grad_txt = together(back_last, up_grad_txt)
    grad_hidden_two = sum_square(back_own, (back_last[0], back_first[0]), (back_first[1], back_last[1]))
    grad_up = [owner_rows(up_grad_img), owner_rows(up_grad_txt)]
    grad_down = [
        lax.psum_scatter(down, ("z", "c"), scatter_dimension=0, tiled=True)
        for down in (down_grad_img, down_grad_txt)
    ]
    grad_after = grad_y + back_normalize(grad_hidden_two * (1.0 + vector(4)), normed_two, spread_two)
    grad_out = (vector(2) * grad_after).astype(BF)

    def token_sums(value):
        return jnp.stack([jnp.sum(value[:, cut].astype(F32), axis=(0, 1)) for cut in streams])

    out_sums, mlp_sums = token_sums(grad_out), token_sums(grad_mlp)
    grad_attn = jnp.concatenate(
        [item.astype(BF) for item in two_streams(grad_out, proj_rel, "bte,de->btd")], 1
    )
    attn_late, grad_attn = together(attn, grad_attn)
    pieces = [grad_attn[:, :, i * rank_cols : (i + 1) * rank_cols] for i in range(4)]
    back = exchange_square(*pieces)
    grad_mixed_seqs = [jnp.concatenate(back[:2], 0), jnp.concatenate(back[2:], 0)]

    def hidden_back(grad_pair):
        return jnp.concatenate(
            [
                jnp.einsum("bte,de->btd", grad_pair[j], qkv_rank[j], preferred_element_type=F32).astype(BF)
                for j in range(2)
            ],
            1,
        )

    (mlp_own, mlp_other), grad_mixed_seqs = together((mlp_own, mlp_other), grad_mixed_seqs)
    mlp_first = relay_square(mlp_other), swap(mlp_other[1:2], "x"), swap(mlp_own[2:3], "y")
    grad_pair_other = attend_backward(*qkv_seqs[1], lse_seqs[1], grad_mixed_seqs[1])
    mlp_first, grad_pair_other = together(mlp_first, grad_pair_other)
    mlp_relays, mlp_x1, mlp_y2 = mlp_first
    hidden_back_other = hidden_back(grad_pair_other)
    mlp_x0 = swap(plus(mlp_other[:1], mlp_relays[0]), "x")
    mlp_y3 = swap(plus(mlp_own[3:4], mlp_relays[1]), "y")

    grad_late, hidden_back_other = together(grad_out, hidden_back_other)
    position = lax.select_n(
        rank ^ jnp.arange(4), *(jnp.full((4,), place, jnp.int32) for place in (0, 2, 1, 3))
    )

    def proj_rows(core):
        blocks = [attn_late[:, :, at * rows : (at + 1) * rows] for at in range(16)]
        left = jnp.concatenate([pick(core, blocks[at], blocks[at + 1]) for at in range(0, 16, 2)], -1)
        return [
            jnp.einsum("btd,bte->de", left[:, cut], grad_late[:, cut], preferred_element_type=F32)
            .astype(BF)
            .reshape(4, 2, rows, width)
            for cut in streams
        ]

    proj_sent, proj_kept = jnp.stack(proj_rows(1 - ci)), jnp.stack(proj_rows(ci))
    proj_received = swap(proj_sent, "c")

    hidden_relays = relay_square(hidden_back_other)
    grad_mixed_own, (hidden_back_other, proj_kept) = together(grad_mixed_seqs[0], (hidden_back_other, proj_kept))
    grad_pair_own = attend_backward(*qkv_seqs[0], lse_seqs[0], grad_mixed_own)
    (hidden_relays, mlp_x0, mlp_y3), grad_pair_own = together((hidden_relays, mlp_x0, mlp_y3), grad_pair_own)
    hidden_back_own = hidden_back(grad_pair_own)
    grad_pairs, hidden_back_own = together([grad_pair_own, grad_pair_other], hidden_back_own)
    hidden_first = swap(hidden_back_other[1:2], "x"), swap(hidden_back_own[2:3], "y")
    hidden_last = (
        swap(plus(hidden_back_other[:1], hidden_relays[0]), "x"),
        swap(plus(hidden_back_own[3:4], hidden_relays[1]), "y"),
    )

    def qkv_grad(j, pairs):
        return two_sums([hid[:, streams[j]] for hid in hidden_seqs], [pair[j] for pair in pairs])

    qkv_grad_img = qkv_grad(0, grad_pairs)
    hidden_first, qkv_grad_img = together(hidden_first, qkv_grad_img)
    (grad_pairs, proj_received), hidden_first = together((grad_pairs, proj_received), hidden_first)
    grad_proj = plus(proj_kept, proj_received)
    grad_proj = jnp.concatenate([lax.dynamic_slice_in_dim(grad_proj, position[t], 1, 1) for t in range(4)], 1)
    proj_kept, proj_received = split_swap(grad_proj, 2, yi, "y")
    qkv_grad_txt = qkv_grad(1, grad_pairs)
    grad_qkv = jnp.stack([qkv_grad_img, qkv_grad_txt])
    cols = grad_qkv.shape[2]
    grad_qkv = grad_qkv.reshape(2, shards, 2, 2, rows, cols).transpose(1, 3, 0, 2, 4, 5)
    grad_qkv = grad_qkv.reshape(2 * shards, 2, 2, rows, cols)
    hidden_last, (grad_qkv, proj_kept) = together(hidden_last, (grad_qkv, proj_kept))
    grad_hidden = sum_square(
        hidden_back_own, (hidden_last[0], hidden_first[0]), (hidden_first[1], hidden_last[1])
    )
    grad_qkv = lax.psum_scatter(grad_qkv, ("z", "c"), scatter_dimension=0, tiled=True).reshape(2, 2, rows, cols)

    (mlp_own, grad_up, grad_down), grad_hidden = together((mlp_own, grad_up, grad_down), grad_hidden)
    mlp = sum_square(mlp_own, (mlp_x0, mlp_x1), (mlp_y2, mlp_y3)) + with_bias(downb_full)
    result = ((after + vector(5) * mlp) * live).astype(BF)
    up_pair = split_swap(replicas(jnp.stack(grad_up)), 1, yi, "y")
    down = replicas(jnp.stack(grad_down))
    down_other = swap(down, "x")
    grad_hidden_late, (up_kept, down) = together(grad_hidden, (up_pair[0], down))
    up_pair = up_kept, up_pair[1]

    grad_tokens = grad_after + back_normalize(grad_hidden * (1.0 + vector(1)), normed, spread_one)

    def from_slot(value):
        return paired(ci, value[:1], swap(value[1:], "c"), 0)

    result = from_slot(result)
    grad_tokens = from_slot(grad_tokens)

    sums = jnp.stack(
        [
            token_sums(grad_hidden_late),
            token_sums(grad_hidden_late * normed),
            token_sums(out * grad_after),
            token_sums(grad_hidden_two),
            token_sums(grad_hidden_two * normed_two),
            token_sums(mlp * grad_y),
        ],
        1,
    ).reshape(2, 6 * width)
    up_pair, sums = together(up_pair, sums)
    up_mine = jnp.concatenate(up_pair, 1)
    dmod = (sums + swap(sums, "y")).astype(BF)
    proj_received, dmod = together(proj_received, dmod)
    proj_kept, proj_received = split_swap(plus(proj_kept, proj_received), 0, xi, "x")
    dmod_rep = spread(dmod, ("z", "c"))
    qkv_pair = split_swap(replicas(grad_qkv), 1, yi, "y")
    (dmod_rep, proj_kept), qkv_kept = together((dmod_rep, proj_kept), qkv_pair[0])
    qkv_pair = qkv_kept, qkv_pair[1]
    grad_proj = plus(proj_kept, proj_received).reshape(shards * rows, width)
    grad_proj = replicas(lax.psum_scatter(grad_proj, "z", scatter_dimension=0, tiled=True))
    g_proj_w = paired(xi, grad_proj[None], swap(grad_proj, "x")[None], 0).astype(F32)
    blocks = (pick(xi, down, down_other), pick(xi, down_other, down))
    g_fc2_w = paired(ci, pick(ci, *blocks), swap(pick(ci, blocks[1], blocks[0]), "c"), 1).astype(F32)
    qkv_mine = jnp.concatenate(qkv_pair, 1)
    g_qkv_w = owner_columns(qkv_mine, swap(qkv_mine, "x"), xi, yi, 3)
    dsilu_part = jnp.einsum("sjm,jdm->sd", dmod_rep, ada_w, preferred_element_type=F32)
    dsilu = spread(dsilu_part, ("z", "y", "c")).transpose(1, 0, 2).reshape(2 * shards, owners * rows)
    gate = jax.nn.sigmoid(cond_value)
    d_cond = dsilu * gate * (1.0 + cond_value * (1.0 - gate))
    dmod_all = spread(dmod_rep, ("x",)).reshape(4 * shards, 2, 6 * width)
    if lax.axis_size("r") > 1:
        dmod_all = lax.all_gather(dmod_all, "r", axis=0, tiled=True)
        silu_all = lax.all_gather(silu_all, "r", axis=0, tiled=True)
    silu_cols = lax.dynamic_slice_in_dim(silu_all, owner * rows, rows, 1)
    g_ada_w = jnp.einsum("sd,sjm->jdm", silu_cols, dmod_all, preferred_element_type=F32)
    g_ada_b = jnp.sum(
        lax.dynamic_slice_in_dim(dmod_all, owner * ada_b.shape[1], ada_b.shape[1], 2).astype(F32), axis=0
    )

    here = ((jnp.arange(2)[:, None] == yi) & (jnp.arange(2)[None] == xi)).astype(F32)
    qkv_sums = (grad_pair_own[2] + grad_pair_other[2]).reshape(2, 3, rank_cols)
    qv_sums = jnp.stack([qkv_sums[:, 0], qkv_sums[:, 2]], 1)
    qv_placed = (qv_sums[:, :, None, None] * here[:, :, None]).reshape(2, 2 * width)
    up_sums = jnp.concatenate([sums_own + sums_other, sums_txt], 0).reshape(2, shards, ff_block)
    up_placed = (up_sums[:, :, None, None] * here[:, :, None]).reshape(2, owners * ff_block)
    biases = jnp.concatenate(
        [qv_placed, out_sums, up_placed, mlp_sums], 1
    )
    biases = replicas(total(biases, ("c", "y", "z", "x")))
    up_mine, biases = together(up_mine, biases)
    g_fc1_w = owner_columns(up_mine, swap(up_mine, "x"), xi, yi, shards)
    g_biases = []
    start = 0
    for item in (qv_b, proj_b, fc1_b, fc2_b):
        cols = item.shape[1]
        g_biases.append(lax.dynamic_slice_in_dim(biases, start + owner * cols, cols, 1))
        start += owners * cols
    return (
        result[:, :img],
        result[:, img:],
        grad_tokens[:, :img],
        grad_tokens[:, img:],
        d_cond,
        g_ada_w,
        g_ada_b,
        g_qkv_w,
        g_biases[0],
        g_proj_w,
        g_biases[1],
        g_fc1_w,
        g_biases[2],
        g_fc2_w,
        g_biases[3],
    )


def solution(mesh):
    reps, shards, seqs = mesh.shape["rep"], mesh.shape["shard"], mesh.shape["seq"]
    fine = Mesh(mesh.devices.reshape(reps // 2, 2, shards, seqs // 2, 2), ("r", "x", "z", "y", "c"))
    group = ("r", "x", "z")
    token = P(group, ("y", "c"), None)
    cond = P(("r", "x"), None)
    matrix = P(None, ("z", "y", "c"), None)
    vector = P(None, ("z", "y", "c"))
    return jax.shard_map(
        on_device,
        mesh=fine,
        in_specs=(token, token, cond, P(group), token, token) + (matrix, vector) * 5,
        out_specs=(token, token, token, token, cond) + (matrix, vector) * 5,
        check_vma=False,
    )
```

```python
import jax
import jax.numpy as jnp
from jax import lax
from jax.experimental import pallas as pl
from jax.experimental.pallas import tpu as pltpu
from jax.sharding import Mesh, PartitionSpec as P

HD = 64
LOG2E = 1.4426950408889634
BF = jnp.bfloat16
F32 = jnp.float32
FLIP = ((0, 1), (1, 0))


def matmul(left, right, left_dim, right_dim):
    return lax.dot_general(
        left, right, (((left_dim,), (right_dim,)), ((), ())), preferred_element_type=F32
    )


def join_streams(img_ref, txt_ref, cut):
    img = img_ref[:, :, cut]
    txt = txt_ref[:, :, cut]
    return jnp.concatenate([img.reshape(-1, HD), txt.reshape(-1, HD)], 0)


def attend_forward_kernel(img_ref, txt_ref, out_ref, lse_ref, *, heads, scale):
    blocks = img_ref.shape[0]
    width = heads * HD
    rows = out_ref.shape[1]
    for head in range(heads):
        cut = slice(head * HD, head * HD + HD)
        keys = join_streams(img_ref, txt_ref, slice(width + cut.start, width + cut.stop))
        values_t = join_streams(img_ref, txt_ref, slice(2 * width + cut.start, 2 * width + cut.stop)).T
        for block in range(blocks):
            queries = jnp.concatenate([img_ref[block, :, cut], txt_ref[block, :, cut]], 0)
            raw = matmul(keys, queries, 1, 1) * scale
            top = jnp.max(raw, axis=0, keepdims=True)
            grown = jnp.exp2(raw - top)
            total = jnp.sum(grown, axis=0, keepdims=True)
            mixed_t = matmul(values_t, grown.astype(BF), 1, 0) * (1.0 / total)
            out_ref[block, :, cut] = mixed_t.T.astype(BF)
            lse_ref[head : head + 1, block * rows : (block + 1) * rows] = top + jnp.log2(total)


def attend_backward_kernel(
    img_ref, txt_ref, lse_ref, grad_ref, img_out, txt_out, sums_out, key_sum, value_sum, *, heads, scale
):
    blocks, img_rows = img_ref.shape[:2]
    txt_rows = txt_ref.shape[1]
    width = heads * HD
    rows = grad_ref.shape[1]
    for head in range(heads):
        cut = slice(head * HD, head * HD + HD)
        key_cut = slice(width + cut.start, width + cut.stop)
        value_cut = slice(2 * width + cut.start, 2 * width + cut.stop)
        keys = join_streams(img_ref, txt_ref, key_cut)
        values = join_streams(img_ref, txt_ref, value_cut)
        keys_t = keys.T
        query_sums = [0.0, 0.0]
        for block in range(blocks):
            queries = jnp.concatenate([img_ref[block, :, cut], txt_ref[block, :, cut]], 0)
            grad = grad_ref[block, :, cut]
            raw = matmul(keys, queries, 1, 1)
            prob = jnp.exp2(raw * scale - lse_ref[head : head + 1, block * rows : (block + 1) * rows])
            value_part = matmul(prob.astype(BF), grad, 1, 0)
            grad_prob = matmul(values, grad, 1, 1)
            delta = jnp.sum(prob * grad_prob, axis=0, keepdims=True)
            grad_raw = (prob * (grad_prob - delta)).astype(BF)
            key_part = matmul(grad_raw, queries, 1, 0)
            if block == 0:
                value_sum[...] = value_part
                key_sum[...] = key_part
            else:
                value_sum[...] += value_part
                key_sum[...] += key_part
            grad_query = (matmul(keys_t, grad_raw, 1, 0) * HD**-0.5).T.astype(BF)
            img_out[block, :, cut] = grad_query[:img_rows]
            txt_out[block, :, cut] = grad_query[img_rows:]
            grad_query = grad_query.astype(F32)
            query_sums[0] += jnp.sum(grad_query[:img_rows], axis=0, keepdims=True)
            query_sums[1] += jnp.sum(grad_query[img_rows:], axis=0, keepdims=True)
        rounded = value_sum[...].astype(BF).astype(F32)
        value_sums = (
            jnp.sum(rounded[: blocks * img_rows], axis=0, keepdims=True),
            jnp.sum(rounded[blocks * img_rows :], axis=0, keepdims=True),
        )
        for stream in range(2):
            sums_out[stream : stream + 1, cut] = query_sums[stream]
            sums_out[stream : stream + 1, key_cut] = jnp.zeros((1, HD), F32)
            sums_out[stream : stream + 1, value_cut] = value_sums[stream]
        for there, total, factor in ((key_cut, key_sum, HD**-0.5), (value_cut, value_sum, 1.0)):
            for block in range(blocks):
                img_out[block, :, there] = (total[block * img_rows : (block + 1) * img_rows] * factor).astype(BF)
                at = blocks * img_rows + block * txt_rows
                txt_out[block, :, there] = (total[at : at + txt_rows] * factor).astype(BF)


def whole(shape):
    return pl.BlockSpec(shape, lambda: (0,) * len(shape))


def attend_cost(img, txt, heads, products):
    length = img.shape[0] * (img.shape[1] + txt.shape[1])
    return pl.CostEstimate(
        flops=products * 18 * heads * length * length * HD,
        bytes_accessed=4 * (img.size + txt.size),
        transcendentals=heads * length * length,
    )


def attend_forward(img, txt):
    blocks = img.shape[0]
    rows = img.shape[1] + txt.shape[1]
    heads = img.shape[2] // (3 * HD)
    outs = ((blocks, rows, heads * HD), (heads, blocks * rows))
    return pl.pallas_call(
        lambda *refs: attend_forward_kernel(*refs, heads=heads, scale=HD**-0.5 * LOG2E),
        in_specs=[whole(img.shape), whole(txt.shape)],
        out_specs=[whole(shape) for shape in outs],
        out_shape=[jax.ShapeDtypeStruct(outs[0], BF), jax.ShapeDtypeStruct(outs[1], F32)],
        compiler_params=pltpu.CompilerParams(vmem_limit_bytes=40 << 20),
        cost_estimate=attend_cost(img, txt, heads, 2),
        name="attend_forward",
    )(img, txt)


def attend_backward(img, txt, lse, grad):
    heads = img.shape[2] // (3 * HD)
    length = img.shape[0] * (img.shape[1] + txt.shape[1])
    return pl.pallas_call(
        lambda *refs: attend_backward_kernel(*refs, heads=heads, scale=HD**-0.5 * LOG2E),
        in_specs=[whole(value.shape) for value in (img, txt, lse, grad)],
        out_specs=[whole(img.shape), whole(txt.shape), whole((2, img.shape[2]))],
        out_shape=[
            jax.ShapeDtypeStruct(img.shape, BF),
            jax.ShapeDtypeStruct(txt.shape, BF),
            jax.ShapeDtypeStruct((2, img.shape[2]), F32),
        ],
        scratch_shapes=[pltpu.VMEM((length, HD), F32), pltpu.VMEM((length, HD), F32)],
        compiler_params=pltpu.CompilerParams(vmem_limit_bytes=40 << 20),
        cost_estimate=attend_cost(img, txt, heads, 5),
        name="attend_backward",
    )(img, txt, lse, grad)


CURVE = 0.7978845608028654
CUBIC = 0.044715


def gelu_and_slope(value):
    square = value * value
    bend = jnp.tanh(CURVE * value * (1.0 + CUBIC * square))
    rise = 0.5 + 0.5 * bend
    slope = rise + 0.5 * CURVE * value * (1.0 - bend * bend) * (1.0 + 3.0 * CUBIC * square)
    return value * rise, slope


def rows_of(refs):
    values = [ref[...].reshape(-1, ref.shape[2]) for ref in refs]
    return values[0] if len(values) == 1 else jnp.concatenate(values, 0)


def store_rows(refs, value):
    start = 0
    for ref in refs:
        stop = start + ref.shape[0] * ref.shape[1]
        ref[...] = value[start:stop].reshape(ref.shape)
        start = stop


def hidden_kernel(*refs, count):
    hids, tops, (up_ref, down_ref, bias_ref) = refs[:count], refs[count : 2 * count], refs[2 * count : 2 * count + 3]
    acts, grads, sums_ref = refs[2 * count + 3 : 3 * count + 3], refs[3 * count + 3 : -1], refs[-1]
    pre = matmul(rows_of(hids), up_ref[...], 1, 0) + bias_ref[...]
    grad_act = matmul(rows_of(tops), down_ref[...], 1, 1)
    act, slope = gelu_and_slope(pre)
    store_rows(acts, act.astype(BF))
    grad_pre = (grad_act * slope).astype(BF)
    store_rows(grads, grad_pre)
    sums_ref[...] = jnp.sum(grad_pre.astype(F32), axis=0, keepdims=True)


def output_kernel(*refs, count):
    acts, grads, (up_ref, down_ref) = refs[:count], refs[count : 2 * count], refs[2 * count : 2 * count + 2]
    mlps, backs = refs[-2 * count : -count], refs[-count:]
    store_rows(backs, matmul(rows_of(grads), up_ref[...], 1, 1).astype(BF))
    store_rows(mlps, matmul(rows_of(acts), down_ref[...], 1, 0).astype(BF))


def feed_forward_hidden(hids, tops, up, down, bias, cut):
    count = len(hids)
    blocks, _, width = hids[0].shape
    rows = cut.stop - cut.start
    ff = up.shape[1]
    tile = 256 if ff % 256 == 0 else ff
    token = pl.BlockSpec((blocks, rows, width), lambda f: (0, cut.start // rows, 0))
    out_spec = pl.BlockSpec((blocks, rows, tile), lambda f: (0, 0, f))
    size = count * blocks * rows
    outs = pl.pallas_call(
        lambda *refs: hidden_kernel(*refs, count=count),
        grid=(ff // tile,),
        in_specs=[
            *[token] * (2 * count),
            pl.BlockSpec((width, tile), lambda f: (0, f)),
            pl.BlockSpec((tile, width), lambda f: (f, 0)),
            pl.BlockSpec((1, tile), lambda f: (0, f)),
        ],
        out_specs=[*[out_spec] * (2 * count), pl.BlockSpec((1, tile), lambda f: (0, f))],
        out_shape=[
            *[jax.ShapeDtypeStruct((blocks, rows, ff), BF)] * (2 * count),
            jax.ShapeDtypeStruct((1, ff), F32),
        ],
        compiler_params=pltpu.CompilerParams(vmem_limit_bytes=48 << 20),
        cost_estimate=pl.CostEstimate(
            flops=8 * size * width * ff, bytes_accessed=4 * size * (width + ff) + 4 * up.size, transcendentals=size * ff
        ),
        name="feed_forward_hidden",
    )(*hids, *tops, up, down, bias)
    return outs[:count], outs[count : 2 * count], outs[-1]


def feed_forward_output(acts, grads, up, down, cut, filled, all_rows):
    count = len(acts)
    blocks, rows, ff = acts[0].shape
    width = up.shape[0]
    tile = 256 if width % 256 == 0 else width
    token = pl.BlockSpec((blocks, rows, ff), lambda n: (0, 0, 0))
    out_spec = pl.BlockSpec((blocks, rows, tile), lambda n: (0, cut.start // rows, n))
    size = count * blocks * rows
    outs = pl.pallas_call(
        lambda *refs: output_kernel(*refs, count=count),
        grid=(width // tile,),
        in_specs=[
            *[token] * (2 * count),
            pl.BlockSpec((tile, ff), lambda n: (n, 0)),
            pl.BlockSpec((ff, tile), lambda n: (0, n)),
            *(pl.BlockSpec(memory_space=pl.ANY) for _ in filled),
        ],
        out_specs=[out_spec] * (2 * count),
        out_shape=[jax.ShapeDtypeStruct((blocks, all_rows, width), BF)] * (2 * count),
        input_output_aliases={2 * count + 2 + at: at for at in range(len(filled))},
        compiler_params=pltpu.CompilerParams(vmem_limit_bytes=48 << 20),
        cost_estimate=pl.CostEstimate(
            flops=8 * size * width * ff, bytes_accessed=4 * size * (width + ff) + 4 * up.size, transcendentals=0
        ),
        name="feed_forward_output",
    )(*acts, *grads, up, down, *filled)
    return outs[:count], outs[count:]


def weight_grad_kernel(*refs, count):
    lefts, rights, out_ref, turned = refs[:count], refs[count : 2 * count], refs[2 * count], refs[2 * count + 1]
    rows = lefts[0].shape[0] * lefts[0].shape[1]

    @pl.when(pl.program_id(0) == 0)
    def _():
        for at, left in enumerate(lefts):
            turned[:, at * rows : (at + 1) * rows] = left[...].reshape(rows, left.shape[2]).T

    total = matmul(turned[:, :rows], rights[0][...].reshape(rows, -1), 1, 0)
    for at in range(1, count):
        total = total + matmul(turned[:, at * rows : (at + 1) * rows], rights[at][...].reshape(rows, -1), 1, 0)
    out_ref[...] = total.astype(BF)


def weight_grad(lefts, rights, left_cut, right_cut):
    count = len(lefts)

    def rows_and_place(value, cut):
        rows = value.shape[1] if cut is None else cut.stop - cut.start
        return rows, 0 if cut is None else cut.start // rows

    blocks, _, left_cols = lefts[0].shape
    right_cols = rights[0].shape[2]
    rows, left_at = rows_and_place(lefts[0], left_cut)
    _, right_at = rows_and_place(rights[0], right_cut)
    tile = next(tile for tile in (512, 384, right_cols) if right_cols % tile == 0)
    tokens = count * blocks * rows
    return pl.pallas_call(
        lambda *refs: weight_grad_kernel(*refs, count=count),
        grid=(right_cols // tile,),
        in_specs=[
            *[pl.BlockSpec((blocks, rows, left_cols), lambda n: (0, left_at, 0))] * count,
            *[pl.BlockSpec((blocks, rows, tile), lambda n: (0, right_at, n))] * count,
        ],
        out_specs=pl.BlockSpec((left_cols, tile), lambda n: (0, n)),
        out_shape=jax.ShapeDtypeStruct((left_cols, right_cols), BF),
        scratch_shapes=[pltpu.VMEM((left_cols, tokens), BF)],
        compiler_params=pltpu.CompilerParams(vmem_limit_bytes=48 << 20),
        cost_estimate=pl.CostEstimate(
            flops=3 * tokens * left_cols * right_cols,
            bytes_accessed=2 * tokens * (left_cols + right_cols) + 2 * left_cols * right_cols,
            transcendentals=0,
        ),
        name="weight_grad",
    )(*lefts, *rights)


def owner_kernel(place_ref, mine_ref, others_ref, out_ref):
    block = mine_ref.shape[3]
    for rank in range(4):
        y = (rank // 2 + place_ref[1]) % 2
        piece = jnp.where(rank % 2 == place_ref[0], mine_ref[:, y], others_ref[:, y])
        out_ref[:, :, rank * block : (rank + 1) * block] = piece.astype(F32)


def owner_columns(mine, others, xi, yi, parts):
    streams, _, rows, cols = mine.shape
    block = cols // parts
    place = jnp.stack([xi, yi]).astype(jnp.int32)
    spec = pl.BlockSpec((streams, 2, rows, block), lambda part, place: (0, 0, 0, part))
    return pl.pallas_call(
        owner_kernel,
        grid_spec=pltpu.PrefetchScalarGridSpec(
            num_scalar_prefetch=1,
            grid=(parts,),
            in_specs=[spec, spec],
            out_specs=pl.BlockSpec((streams, rows, 4 * block), lambda part, place: (0, 0, part)),
        ),
        out_shape=jax.ShapeDtypeStruct((streams, rows, 4 * cols), F32),
        compiler_params=pltpu.CompilerParams(vmem_limit_bytes=32 << 20),
        cost_estimate=pl.CostEstimate(flops=0, bytes_accessed=24 * mine.size, transcendentals=0),
        name="owner_columns",
    )(place, mine, others)


def swap(value, axis):
    return lax.ppermute(value, axis, FLIP)


def shift_xor(value, axis, bit):
    return lax.ppermute(value, axis, [(i, i ^ bit) for i in range(lax.axis_size(axis))])


def shift(value, axis, step):
    size = lax.axis_size(axis)
    return lax.ppermute(value, axis, [(i, (i + step) % size) for i in range(size)])


def swap_both(value):
    return lax.ppermute(value, ("x", "y"), [(i, 3 - i) for i in range(4)])


def pick(index, first, second):
    return jnp.where(index == 0, first, second)


def paired(index, own, other, axis):
    return jnp.where(
        index == 0, jnp.concatenate([own, other], axis), jnp.concatenate([other, own], axis)
    )


def split_swap(value, dim, index, axis):
    first, second = jnp.split(value, 2, axis=dim)
    return pick(index, first, second), swap(pick(index, second, first), axis)


def spread(value, axes):
    value = value[None]
    for axis in reversed(axes):
        size, here = lax.axis_size(axis), lax.axis_index(axis)
        bit = 1
        while bit < size:
            value = paired((here // bit) % 2, value, shift_xor(value, axis, bit), 0)
            bit *= 2
    return value


def total(value, axes):
    for axis in axes:
        bit = 1
        while bit < lax.axis_size(axis):
            value = value + shift_xor(value, axis, bit)
            bit *= 2
    return value


def together(values, others):
    return lax.optimization_barrier((values, others))


def gather_square(own):
    from_x, from_y = swap(own, "x"), swap(own, "y")
    corner_a, corner_b = swap(from_x[:1], "y"), swap(from_y[1:], "x")
    return jnp.concatenate([own, from_y], 0), jnp.concatenate([from_x, corner_a, corner_b], 0)


def plus(first, second):
    return (first.astype(F32) + second.astype(F32)).astype(BF)


def relay_square(other):
    return swap(other[2:3], "y"), swap(other[3:4], "x")


def send_x(other, relays):
    return swap(plus(other[:1], relays[0]), "x"), swap(other[1:2], "x")


def send_y(own, relays):
    return swap(own[2:3], "y"), swap(plus(own[3:4], relays[1]), "y")


def sum_square(own, from_x, from_y):
    return own[:2].astype(F32) + jnp.concatenate(from_x, 0).astype(F32) + jnp.concatenate(from_y, 0).astype(F32)


def exchange_square(own, for_y, for_x, for_corner):
    return [own, swap(for_y, "y"), swap(for_x, "x"), swap_both(for_corner)]


def on_device(
    x_img,
    x_txt,
    cond,
    counts,
    ct_img,
    ct_txt,
    ada_w,
    ada_b,
    qkv_w,
    qv_b,
    proj_w,
    proj_b,
    fc1_w,
    fc1_b,
    fc2_w,
    fc2_b,
):
    xi, yi, zi, ci = (lax.axis_index(name) for name in ("x", "y", "z", "c"))
    shards = lax.axis_size("z")
    owners = 4 * shards
    owner = zi * 4 + yi * 2 + ci
    width = x_img.shape[2]
    rows = ada_w.shape[1]
    rank_cols = width // 4
    ff_block = fc2_w.shape[1]
    img = x_img.shape[1]
    txt = x_txt.shape[1]
    live = (ci < counts[0]).astype(F32)
    streams = (slice(0, img), slice(img, img + txt))

    def to_slot(img_part, txt_part):
        both = jnp.concatenate([img_part, txt_part], 1)
        kept, received = split_swap(both, 0, ci, "c")
        return jnp.concatenate([kept, received], 0)

    tokens = to_slot(x_img, x_txt).astype(F32)

    cotangents = to_slot(ct_img, ct_txt)
    ct_from_x, ct_from_y = swap(cotangents, "x"), swap(cotangents, "y")

    cond_value = cond.astype(F32)
    silu_cond = jax.nn.silu(cond_value).astype(BF)
    silu_own = lax.dynamic_slice_in_dim(silu_cond, owner * rows, rows, 1).reshape(shards, 2, rows)
    bias_full = lax.dynamic_update_slice_in_dim(
        jnp.zeros((2, 6 * width), F32), ada_b.astype(F32), owner * ada_b.shape[1], 1
    )

    def partial_mod(slots):
        return jnp.einsum("sd,jdm->sjm", slots, ada_w, preferred_element_type=F32) + bias_full

    mod_peer = partial_mod(pick(ci, silu_own[:, 1], silu_own[:, 0]))
    mod_sent = swap(mod_peer, "c")
    mod_own = partial_mod(pick(ci, silu_own[:, 0], silu_own[:, 1]))
    mod = mod_own + mod_sent
    small = spread(jnp.concatenate([qv_b, proj_b, fc1_b, fc2_b], 1), ("z", "c", "y"))
    small, mod = together(small, mod)
    small = small.reshape(shards, 2, 2, 2, -1).swapaxes(1, 2).reshape(owners, 2, -1)
    mod_here = lax.dynamic_index_in_dim(mod, zi, 0, keepdims=False)
    for step in range(1, shards):
        there = lax.dynamic_index_in_dim(mod, (zi + step) % shards, 0, keepdims=False)
        mod_here = mod_here + shift(there, "z", step)
    mod = (mod_here + swap(mod_here, "y")).reshape(2, 6, width)
    stream_of_row = (jnp.arange(img + txt) >= img)[None, :, None]

    def vector(index):
        return jnp.where(stream_of_row, mod[1, index], mod[0, index])

    def with_bias(pair):
        return jnp.where(stream_of_row, pair[1], pair[0])

    def rank_columns(weight, offsets):
        by_y = [
            pick(
                xi,
                *(
                    jnp.concatenate([weight[:, :, at : at + size] for at, size in offsets(y, x)], 2)
                    for x in range(2)
                ),
            )
            for y in range(2)
        ]
        return pick(yi, by_y[0], by_y[1]), swap(pick(yi, by_y[1], by_y[0]), "y")

    def by_owner(kept, received):
        return jnp.stack([pick(yi, kept, received), pick(yi, received, kept)], 1)

    def natural_rows(gathered):
        cols = gathered.shape[3]
        return gathered.reshape(shards, 2, 2, rows, cols).transpose(0, 2, 1, 3, 4).reshape(width, cols)

    def qkv_offsets(y, x):
        return [(third * width + (2 * y + x) * rank_cols, rank_cols) for third in range(3)]

    def up_offsets(y, x):
        return [((z * 4 + y * 2 + x) * ff_block, ff_block) for z in range(shards)]

    qkv_pair = rank_columns(qkv_w, qkv_offsets)
    proj_swapped = swap(proj_w, "y")
    qkv_held = by_owner(*qkv_pair)
    qkv_gathered = lax.all_gather(qkv_held, ("z", "c"), axis=0)
    qkv_rank = [natural_rows(qkv_gathered[:, j]) for j in range(2)]

    def statistics(value):
        centre = jnp.mean(value, axis=-1, keepdims=True)
        offset = value - centre
        return offset, lax.rsqrt(jnp.mean(offset * offset, axis=-1, keepdims=True) + 1e-06)

    def back_normalize(grad, normed, scale):
        return scale * (
            grad
            - jnp.mean(grad, axis=-1, keepdims=True)
            - normed * jnp.mean(grad * normed, axis=-1, keepdims=True)
        )

    offset, spread_one = statistics(tokens)
    normed = offset * spread_one
    hidden = (normed * (1.0 + vector(1)) + vector(0)).astype(BF)
    gate_live = mod[:, 5] * live
    gate_other = swap(gate_live, "x")
    hidden_x, hidden_y = swap(hidden, "x"), swap(hidden, "y")
    (ct_from_x, ct_from_y), (hidden_x, hidden_y) = together((ct_from_x, ct_from_y), (hidden_x, hidden_y))
    hidden_corner = swap(hidden_x[:1], "y"), swap(hidden_y[1:], "x")
    ct_corner = swap(ct_from_x[:1], "y"), swap(ct_from_y[1:], "x")
    hidden_seqs = [
        jnp.concatenate([hidden, hidden_y], 0),
        jnp.concatenate([hidden_x, *hidden_corner], 0),
    ]

    proj_held = by_owner(proj_w, proj_swapped)
    (fc1_w, fc2_w), hidden_seqs = together((fc1_w, fc2_w), hidden_seqs)
    up_pair = rank_columns(fc1_w, up_offsets)

    cuts = [0]
    for item in (qv_b, proj_b, fc1_b, fc2_b):
        cuts.append(cuts[-1] + item.shape[1])
    qv_full, projb_full, upb_full, downb_full = (
        small[:, :, cuts[i] : cuts[i + 1]].transpose(1, 0, 2).reshape(2, -1).astype(F32) for i in range(4)
    )

    def at_rank(pieces):
        return pick(yi, pick(xi, *pieces[0]), pick(xi, *pieces[1]))

    def rank_vector(value, offsets):
        return at_rank(
            [
                [jnp.concatenate([value[:, at : at + size] for at, size in offsets(y, x)], 1) for x in range(2)]
                for y in range(2)
            ]
        )

    qv_rank = rank_vector(qv_full, lambda y, x: qkv_offsets(y, x)[:2])
    qkv_bias = jnp.concatenate(
        [qv_rank[:, :rank_cols], jnp.zeros((2, rank_cols), F32), qv_rank[:, rank_cols:]], 1
    )
    up_bias = rank_vector(upb_full, up_offsets)

    proj_gathered = lax.all_gather(proj_held, ("z", "c"), axis=0).reshape(shards, 2, 2, 2, rows, width)
    def two_streams(value, weights, equation):
        return [
            jnp.einsum(equation, value[:, cut], weights[j], preferred_element_type=F32)
            for j, cut in enumerate(streams)
        ]

    halves = jnp.split(fc2_w, 2, axis=1)
    down_sent = swap(pick(ci, halves[1], halves[0]), "c")
    qkv_seqs, mixed_seqs, lse_seqs = [], [], []
    for value in hidden_seqs:
        if mixed_seqs:
            value, mixed_seqs = together(value, mixed_seqs)
        pair = [
            (item + qkv_bias[j]).astype(BF)
            for j, item in enumerate(two_streams(value, qkv_rank, "btd,de->bte"))
        ]
        if not mixed_seqs:
            up_pair, pair = together(up_pair, pair)
            up_held = by_owner(*up_pair)
        mixed, lse = attend_forward(*pair)
        qkv_seqs.append(pair)
        mixed_seqs.append(mixed)
        lse_seqs.append(lse)
    down_held = jnp.where(ci == xi, pick(ci, halves[0], halves[1]), down_sent)

    def gather_up(piece):
        return natural_rows(lax.all_gather(piece, ("z", "c"), axis=0))

    def gather_down(piece):
        return lax.all_gather(piece, ("z", "c"), axis=0, tiled=True)

    up_img = gather_up(up_held[0])
    down_img = gather_down(down_held[0])
    attn = jnp.concatenate(
        exchange_square(mixed_seqs[0][:2], mixed_seqs[0][2:], mixed_seqs[1][:2], mixed_seqs[1][2:]), -1
    )
    up_rank = [up_img, gather_up(up_held[1])]
    rank = 2 * yi + xi
    relative = (0, 2, 1, 3)
    proj_rel = [
        jnp.concatenate(
            [
                lax.dynamic_index_in_dim(proj_gathered, rank ^ flip, 0, keepdims=False)[:, j]
                .transpose(1, 0, 2, 3)
                .reshape(rank_cols, width)
                for flip in relative
            ],
            0,
        )
        for j in range(2)
    ]
    out = jnp.concatenate(two_streams(attn, proj_rel, "btd,de->bte"), 1) + with_bias(projb_full)
    after = tokens + vector(2) * out

    offset_two, spread_two = statistics(after)
    normed_two = offset_two * spread_two
    hidden_two = (normed_two * (1.0 + vector(4)) + vector(3)).astype(BF)
    (silu_cond, cotangents, ct_from_x, ct_corner), hidden_two = together(
        (silu_cond, cotangents, ct_from_x, ct_corner), hidden_two
    )
    silu_all = spread(silu_cond, ("x",)).reshape(4 * shards, width)
    grad_y = cotangents.astype(F32) * live

    def gated(gate, blocks):
        return (jnp.where(stream_of_row, gate[1], gate[0]) * jnp.concatenate(blocks, 0).astype(F32)).astype(BF)

    grad_mlp_seqs = [
        gated(gate_live, (cotangents, ct_from_y)),
        gated(gate_other, (ct_from_x, *ct_corner)),
    ]
    grad_mlp = grad_mlp_seqs[0][:2]
    down_rank = [down_img, gather_down(down_held[1])]
    hidden_two_seqs = gather_square(hidden_two)
    rows_all = img + txt

    def hidden_of(j, hids, tops):
        return feed_forward_hidden(hids, tops, up_rank[j], down_rank[j], up_bias[j : j + 1], streams[j])

    def output_of(j, acts, pres, filled):
        return feed_forward_output(acts, pres, up_rank[j], down_rank[j], streams[j], filled, rows_all)

    act_img_other, pre_img_other, sums_other = hidden_of(0, hidden_two_seqs[1:], grad_mlp_seqs[1:])
    mlp_other, back_other = output_of(0, act_img_other, pre_img_other, ())
    act_img_own, pre_img_own, sums_own = hidden_of(0, hidden_two_seqs[:1], grad_mlp_seqs[:1])
    mlp_own, back_own = output_of(0, act_img_own, pre_img_own, ())
    act_img, pre_img = [*act_img_own, *act_img_other], [*pre_img_own, *pre_img_other]
    act_txt, pre_txt, sums_txt = hidden_of(1, hidden_two_seqs, grad_mlp_seqs)
    (mlp_own, mlp_other), (back_own, back_other) = output_of(
        1, act_txt, pre_txt, (*mlp_own, *mlp_other, *back_own, *back_other)
    )
    (pre_img, act_txt, pre_txt), (back_own, back_other) = together((pre_img, act_txt, pre_txt), (back_own, back_other))
    back_relays = relay_square(back_other)
    back_first = swap(back_other[1:2], "x"), swap(back_own[2:3], "y")

    def replicas(value):
        return lax.psum(value, "r") if lax.axis_size("r") > 1 else value

    def two_sums(lefts, rights):
        first, second = (
            jnp.einsum("btd,bte->de", left, right, preferred_element_type=F32) for left, right in zip(lefts, rights)
        )
        return (first + second).astype(BF)

    def owner_rows(grad):
        cols = grad.shape[1]
        value = grad.reshape(shards, 2, 2, rows, cols).transpose(0, 2, 1, 3, 4).reshape(-1, cols)
        return lax.psum_scatter(value, ("z", "c"), scatter_dimension=0, tiled=True).reshape(2, rows, cols)

    cut = streams[0]
    down_grad_img = two_sums(act_img, [top[:, cut] for top in grad_mlp_seqs])
    up_grad_img = two_sums([hid[:, cut] for hid in hidden_two_seqs], pre_img)
    down_grad_txt = weight_grad(act_txt, grad_mlp_seqs, None, streams[1])
    (back_relays, back_first), (up_grad_img, down_grad_txt) = together(
        (back_relays, back_first), (up_grad_img, down_grad_txt)
    )
    pre_txt, back_relays = together(pre_txt, back_relays)
    back_last = swap(plus(back_other[:1], back_relays[0]), "x"), swap(plus(back_own[3:4], back_relays[1]), "y")
    up_grad_txt = weight_grad(hidden_two_seqs, pre_txt, streams[1], None)
    back_last, (up_grad_txt, down_grad_img) = together(back_last, (up_grad_txt, down_grad_img))
    grad_hidden_two = sum_square(back_own, (back_last[0], back_first[0]), (back_first[1], back_last[1]))
    grad_up = [owner_rows(up_grad_img), owner_rows(up_grad_txt)]
    grad_down = [
        lax.psum_scatter(down, ("z", "c"), scatter_dimension=0, tiled=True)
        for down in (down_grad_img, down_grad_txt)
    ]
    grad_after = grad_y + back_normalize(grad_hidden_two * (1.0 + vector(4)), normed_two, spread_two)
    grad_out = (vector(2) * grad_after).astype(BF)

    def token_sums(value):
        return jnp.stack([jnp.sum(value[:, cut].astype(F32), axis=(0, 1)) for cut in streams])

    out_sums, mlp_sums = token_sums(grad_out), token_sums(grad_mlp)
    grad_attn = jnp.concatenate(
        [item.astype(BF) for item in two_streams(grad_out, proj_rel, "bte,de->btd")], 1
    )
    attn_late, grad_attn = together(attn, grad_attn)
    pieces = [grad_attn[:, :, i * rank_cols : (i + 1) * rank_cols] for i in range(4)]
    back = exchange_square(*pieces)
    grad_mixed_seqs = [jnp.concatenate(back[:2], 0), jnp.concatenate(back[2:], 0)]

    def hidden_back(grad_pair):
        return jnp.concatenate(
            [
                jnp.einsum("bte,de->btd", grad_pair[j], qkv_rank[j], preferred_element_type=F32).astype(BF)
                for j in range(2)
            ],
            1,
        )

    (mlp_own, mlp_other), grad_mixed_seqs = together((mlp_own, mlp_other), grad_mixed_seqs)
    mlp_first = relay_square(mlp_other), swap(mlp_other[1:2], "x"), swap(mlp_own[2:3], "y")
    grad_pair_other = attend_backward(*qkv_seqs[1], lse_seqs[1], grad_mixed_seqs[1])
    mlp_first, grad_pair_other = together(mlp_first, grad_pair_other)
    mlp_relays, mlp_x1, mlp_y2 = mlp_first
    hidden_back_other = hidden_back(grad_pair_other)
    mlp_x0 = swap(plus(mlp_other[:1], mlp_relays[0]), "x")
    mlp_y3 = swap(plus(mlp_own[3:4], mlp_relays[1]), "y")

    grad_late, hidden_back_other = together(grad_out, hidden_back_other)
    position = lax.select_n(
        rank ^ jnp.arange(4), *(jnp.full((4,), place, jnp.int32) for place in (0, 2, 1, 3))
    )

    def proj_rows(core):
        blocks = [attn_late[:, :, at * rows : (at + 1) * rows] for at in range(16)]
        left = jnp.concatenate([pick(core, blocks[at], blocks[at + 1]) for at in range(0, 16, 2)], -1)
        return [
            jnp.einsum("btd,bte->de", left[:, cut], grad_late[:, cut], preferred_element_type=F32)
            .astype(BF)
            .reshape(4, 2, rows, width)
            for cut in streams
        ]

    proj_sent, proj_kept = jnp.stack(proj_rows(1 - ci)), jnp.stack(proj_rows(ci))
    proj_received = swap(proj_sent, "c")

    hidden_relays = relay_square(hidden_back_other)
    grad_mixed_own, (hidden_back_other, proj_kept) = together(grad_mixed_seqs[0], (hidden_back_other, proj_kept))
    grad_pair_own = attend_backward(*qkv_seqs[0], lse_seqs[0], grad_mixed_own)
    (hidden_relays, mlp_x0, mlp_y3), grad_pair_own = together((hidden_relays, mlp_x0, mlp_y3), grad_pair_own)
    hidden_back_own = hidden_back(grad_pair_own)
    grad_pairs, hidden_back_own = together([grad_pair_own, grad_pair_other], hidden_back_own)
    hidden_first = swap(hidden_back_other[1:2], "x"), swap(hidden_back_own[2:3], "y")
    hidden_last = (
        swap(plus(hidden_back_other[:1], hidden_relays[0]), "x"),
        swap(plus(hidden_back_own[3:4], hidden_relays[1]), "y"),
    )

    def qkv_grad(j, pairs):
        return two_sums([hid[:, streams[j]] for hid in hidden_seqs], [pair[j] for pair in pairs])

    qkv_grad_img = qkv_grad(0, grad_pairs)
    hidden_first, qkv_grad_img = together(hidden_first, qkv_grad_img)
    (grad_pairs, proj_received, grad_up), hidden_first = together((grad_pairs, proj_received, grad_up), hidden_first)
    up_pair = split_swap(replicas(jnp.stack(grad_up)), 1, yi, "y")
    proj_received, up_kept = together(proj_received, up_pair[0])
    grad_proj = plus(proj_kept, proj_received)
    grad_proj = jnp.concatenate([lax.dynamic_slice_in_dim(grad_proj, position[t], 1, 1) for t in range(4)], 1)
    proj_kept, proj_received = split_swap(grad_proj, 2, yi, "y")
    qkv_grad_txt = qkv_grad(1, grad_pairs)
    grad_qkv = jnp.stack([qkv_grad_img, qkv_grad_txt])
    cols = grad_qkv.shape[2]
    grad_qkv = grad_qkv.reshape(2, shards, 2, 2, rows, cols).transpose(1, 3, 0, 2, 4, 5)
    grad_qkv = grad_qkv.reshape(2 * shards, 2, 2, rows, cols)
    (hidden_last, up_received), (grad_qkv, proj_kept) = together((hidden_last, up_pair[1]), (grad_qkv, proj_kept))
    up_mine = jnp.concatenate([up_kept, up_received], 1)
    grad_hidden = sum_square(
        hidden_back_own, (hidden_last[0], hidden_first[0]), (hidden_first[1], hidden_last[1])
    )
    grad_qkv = lax.psum_scatter(grad_qkv, ("z", "c"), scatter_dimension=0, tiled=True).reshape(2, 2, rows, cols)

    (mlp_own, up_mine, grad_down, late_sums), grad_hidden = together(
        (mlp_own, up_mine, grad_down, (sums_own, sums_other, sums_txt)), grad_hidden
    )
    sums_own, sums_other, sums_txt = late_sums
    mlp = sum_square(mlp_own, (mlp_x0, mlp_x1), (mlp_y2, mlp_y3)) + with_bias(downb_full)
    result = ((after + vector(5) * mlp) * live).astype(BF)
    down = replicas(jnp.stack(grad_down))
    down_other = swap(down, "x")
    grad_hidden_late, down = together(grad_hidden, down)

    grad_tokens = grad_after + back_normalize(grad_hidden * (1.0 + vector(1)), normed, spread_one)

    def from_slot(value):
        return paired(ci, value[:1], swap(value[1:], "c"), 0)

    result = from_slot(result)
    grad_tokens = from_slot(grad_tokens)

    sums = jnp.stack(
        [
            token_sums(grad_hidden_late),
            token_sums(grad_hidden_late * normed),
            token_sums(out * grad_after),
            token_sums(grad_hidden_two),
            token_sums(grad_hidden_two * normed_two),
            token_sums(mlp * grad_y),
        ],
        1,
    ).reshape(2, 6 * width)
    dmod = (sums + swap(sums, "y")).astype(BF)
    proj_received, dmod = together(proj_received, dmod)
    proj_kept, proj_received = split_swap(plus(proj_kept, proj_received), 0, xi, "x")
    dmod_rep = spread(dmod, ("z", "c"))
    qkv_pair = split_swap(replicas(grad_qkv), 1, yi, "y")
    (dmod_rep, proj_kept), qkv_kept = together((dmod_rep, proj_kept), qkv_pair[0])
    qkv_pair = qkv_kept, qkv_pair[1]
    grad_proj = plus(proj_kept, proj_received).reshape(shards * rows, width)
    grad_proj = replicas(lax.psum_scatter(grad_proj, "z", scatter_dimension=0, tiled=True))
    g_proj_w = paired(xi, grad_proj[None], swap(grad_proj, "x")[None], 0).astype(F32)
    blocks = (pick(xi, down, down_other), pick(xi, down_other, down))
    g_fc2_w = paired(ci, pick(ci, *blocks), swap(pick(ci, blocks[1], blocks[0]), "c"), 1).astype(F32)
    qkv_mine = jnp.concatenate(qkv_pair, 1)
    g_qkv_w = owner_columns(qkv_mine, swap(qkv_mine, "x"), xi, yi, 3)
    dsilu_part = jnp.einsum("sjm,jdm->sd", dmod_rep, ada_w, preferred_element_type=F32)
    dsilu = spread(dsilu_part, ("z", "y", "c")).transpose(1, 0, 2).reshape(2 * shards, owners * rows)
    gate = jax.nn.sigmoid(cond_value)
    d_cond = dsilu * gate * (1.0 + cond_value * (1.0 - gate))
    dmod_all = spread(dmod_rep, ("x",)).reshape(4 * shards, 2, 6 * width)
    if lax.axis_size("r") > 1:
        dmod_all = lax.all_gather(dmod_all, "r", axis=0, tiled=True)
        silu_all = lax.all_gather(silu_all, "r", axis=0, tiled=True)
    silu_cols = lax.dynamic_slice_in_dim(silu_all, owner * rows, rows, 1)
    g_ada_w = jnp.einsum("sd,sjm->jdm", silu_cols, dmod_all, preferred_element_type=F32)
    g_ada_b = jnp.sum(
        lax.dynamic_slice_in_dim(dmod_all, owner * ada_b.shape[1], ada_b.shape[1], 2).astype(F32), axis=0
    )

    here = ((jnp.arange(2)[:, None] == yi) & (jnp.arange(2)[None] == xi)).astype(F32)
    qkv_sums = (grad_pair_own[2] + grad_pair_other[2]).reshape(2, 3, rank_cols)
    qv_sums = jnp.stack([qkv_sums[:, 0], qkv_sums[:, 2]], 1)
    qv_placed = (qv_sums[:, :, None, None] * here[:, :, None]).reshape(2, 2 * width)
    up_sums = jnp.concatenate([sums_own + sums_other, sums_txt], 0).reshape(2, shards, ff_block)
    up_placed = (up_sums[:, :, None, None] * here[:, :, None]).reshape(2, owners * ff_block)
    biases = jnp.concatenate(
        [qv_placed, out_sums, up_placed, mlp_sums], 1
    )
    biases = replicas(total(biases, ("c", "y", "z", "x")))
    up_mine, biases = together(up_mine, biases)
    g_fc1_w = owner_columns(up_mine, swap(up_mine, "x"), xi, yi, shards)
    g_biases = []
    start = 0
    for item in (qv_b, proj_b, fc1_b, fc2_b):
        cols = item.shape[1]
        g_biases.append(lax.dynamic_slice_in_dim(biases, start + owner * cols, cols, 1))
        start += owners * cols
    return (
        result[:, :img],
        result[:, img:],
        grad_tokens[:, :img],
        grad_tokens[:, img:],
        d_cond,
        g_ada_w,
        g_ada_b,
        g_qkv_w,
        g_biases[0],
        g_proj_w,
        g_biases[1],
        g_fc1_w,
        g_biases[2],
        g_fc2_w,
        g_biases[3],
    )


def solution(mesh):
    reps, shards, seqs = mesh.shape["rep"], mesh.shape["shard"], mesh.shape["seq"]
    fine = Mesh(mesh.devices.reshape(reps // 2, 2, shards, seqs // 2, 2), ("r", "x", "z", "y", "c"))
    group = ("r", "x", "z")
    token = P(group, ("y", "c"), None)
    cond = P(("r", "x"), None)
    matrix = P(None, ("z", "y", "c"), None)
    vector = P(None, ("z", "y", "c"))
    return jax.shard_map(
        on_device,
        mesh=fine,
        in_specs=(token, token, cond, P(group), token, token) + (matrix, vector) * 5,
        out_specs=(token, token, token, token, cond) + (matrix, vector) * 5,
        check_vma=False,
    )
```
